32 devices in a mesh: blk: 8 (over z, core), seq: 4 (over y, x).
Axes of the slice: x: 2, y: 2, z: 4, core: 2. Of those that a mesh axis runs over, the one named last changes fastest.
Arguments:
- activations: bfloat16 [8, 2048, 8192], P('blk', 'seq'), may hold values from -6 to 6
- base_weight: bfloat16 [8192, 1024], P('blk', 'seq'), may hold values from -0.0625 to 0.0625
- adapter_down: bfloat16 [8, 16, 8192], P('blk'), may hold values from -0.0625 to 0.0625
- adapter_up: bfloat16 [8, 16, 1024], P('blk'), may hold values from -1.5 to 1.5
- cotangent: bfloat16 [8, 2048, 1024], P('blk', 'seq'), may hold values from -12 to 12
Outputs:
- projected: bfloat16 [8, 2048, 1024], P('blk', 'seq')
- gradient_inputs: bfloat16 [8, 2048, 8192], P('blk', 'seq')
- down_gradient: float32 [8, 16, 8192], P('blk')
- up_gradient: float32 [8, 16, 1024], P('blk')
The draws below stay inside these ranges and needn't reach their ends.
All inputs are finite; a program needn't handle non-finite values.
Results may differ from the reference program's by a relative error of at most 0.0047.
Values may be sent and summed in bfloat16 or wider, within the bound.
No kernel may reach another device: no remote copies, remote signals or barrier semaphores. Data moves between devices by JAX's collectives and lax.ppermute only.
A program may use at most 128 MiB of HBM per device.

```python
import math
import jax
import jax.numpy as jnp
from jax import lax

D = 8192
KVW = 1024
R = 16
TRIAL_TOKENS = 2048
TRIALS = 8


def draw_cotangent(key, part):
    key_values = jax.random.fold_in(key, 11)
    key_rows = jax.random.fold_in(key, 12)
    position = jnp.arange(TRIAL_TOKENS, dtype=jnp.float32) / max(TRIAL_TOKENS - 1, 1)
    rising = jnp.exp(math.log(3.0) * position)[None, :, None]
    row_factor = jnp.exp(jax.random.uniform(key_rows, (TRIALS, TRIAL_TOKENS, 1), jnp.float32, 0.0, math.log(10.0)))
    values = jnp.clip(jax.random.normal(key_values, (TRIALS, TRIAL_TOKENS, KVW), jnp.float32), -4.0, 4.0)
    return (values * rising * row_factor / 10.0).astype(jnp.bfloat16)


def block_scale(own_key, extent, shards, least, top_value):
    def one(dim, shards_of):
        draws = jax.random.uniform(jax.random.fold_in(jax.random.fold_in(own_key, 6), dim), (shards_of,), jnp.float32, least / len(shards), top_value / len(shards))
        return jnp.repeat(jnp.exp(draws), extent[dim] // shards_of).reshape((-1,) + (1,) * (len(extent) - dim - 1))

    level = one(*shards[0])
    for cut in shards[1:]:
        level = level * one(*cut)
    return level


def noise(stream_key, dims, spread, bound, shards=(), held_as=jnp.bfloat16):
    factor_of = block_scale(stream_key, dims, shards, -0.22, 0.18) if shards else 1.0
    result = jax.random.normal(stream_key, dims, jnp.float32) * spread * factor_of
    return jnp.minimum(jnp.maximum(result, -bound), bound).astype(held_as)


def setup_inputs(seed: int = 0) -> dict:
    arg_keys = jax.random.split(jax.random.key(seed), 6)
    return {
        "activations": noise(arg_keys[0], (TRIALS, TRIAL_TOKENS, D), 1.0, 6.0, ((0, 8), (1, 4))),
        "base_weight": noise(arg_keys[1], (D, KVW), D ** -0.5, 0.0625, ((0, 8), (1, 4))),
        "adapter_down": noise(arg_keys[2], (TRIALS, R, D), D ** -0.5, 0.0625, ((0, 8),)),
        "adapter_up": noise(arg_keys[3], (TRIALS, R, KVW), R ** -0.5, 1.5, ((0, 8),)),
        "cotangent": draw_cotangent(jax.random.fold_in(arg_keys[5], 71), 0),
    }


adapter_scale = 2.0


def reference(activations, base_weight, adapter_down, adapter_up, cotangent):
    def one_trial(inputs):
        token_inputs, down_matrix, up_matrix, output_cotangent = inputs
        lowrank_forward = jnp.dot(token_inputs, down_matrix.T, preferred_element_type=jnp.float32).astype(jnp.bfloat16)
        projected = jnp.dot(token_inputs, base_weight, preferred_element_type=jnp.float32)
        projected = projected + adapter_scale * jnp.dot(lowrank_forward, up_matrix, preferred_element_type=jnp.float32)
        lowrank_backward = jnp.dot(output_cotangent, up_matrix.T, preferred_element_type=jnp.float32).astype(jnp.bfloat16)
        gradient_inputs = jnp.dot(output_cotangent, base_weight.T, preferred_element_type=jnp.float32)
        gradient_inputs = gradient_inputs + adapter_scale * jnp.dot(lowrank_backward, down_matrix, preferred_element_type=jnp.float32)
        down_gradient = (adapter_scale / TRIAL_TOKENS) * jnp.dot(lowrank_backward.T, token_inputs, preferred_element_type=jnp.float32)
        up_gradient = (adapter_scale / TRIAL_TOKENS) * jnp.dot(lowrank_forward.T, output_cotangent, preferred_element_type=jnp.float32)
        return projected.astype(jnp.bfloat16), gradient_inputs.astype(jnp.bfloat16), down_gradient, up_gradient

    return tuple(lax.map(one_trial, (activations, adapter_down, adapter_up, cotangent)))
```

```python
import functools

import jax
import jax.numpy as jnp
import numpy as np
from jax import lax
from jax.experimental import pallas as pl
from jax.experimental.pallas import tpu as pltpu
from jax.sharding import PartitionSpec as P

adapter_scale = 2.0
axes = ("blk", "seq")
f32 = jnp.float32
bf16 = jnp.bfloat16


def dot(a, b, contract):
    return lax.dot_general(a, b, (contract, ((), ())), preferred_element_type=f32)


class Layout:
    def __init__(self, mesh):
        self.blocks, self.seqs = mesh.shape["blk"], mesh.shape["seq"]
        self.depth = self.blocks // 2
        self.cycle = list(range(0, self.seqs, 2)) + list(range(self.seqs - 1, 0, -2))
        self.place = {seq: at for at, seq in enumerate(self.cycle)}
        self.forward_steps = self.seqs // 2
        self.backward_steps = self.seqs - 1 - self.forward_steps
        self.offsets = [0] + list(range(1, self.forward_steps + 1))
        self.offsets += [-step for step in range(1, self.backward_steps + 1)]

    def permute(self, value, target):
        pairs = []
        for blk in range(self.blocks):
            for seq in range(self.seqs):
                to_blk, to_seq = target(blk // 2, blk % 2, seq)
                pairs.append((blk * self.seqs + seq, to_blk * self.seqs + to_seq))
        return lax.ppermute(value, axes, pairs)

    def along_depth(self, value, shift):
        return self.permute(
            value, lambda z, core, seq: (((z + shift) % self.depth) * 2 + core, seq)
        )

    def along_cycle(self, value, step):
        def target(z, core, seq):
            sign = step if core == 0 else -step
            return z * 2 + core, self.cycle[(self.place[seq] + sign) % self.seqs]

        return self.permute(value, target)

    def swap_cores(self, value):
        return self.permute(value, lambda z, core, seq: (z * 2 + 1 - core, seq))

    def column_of(self, core, seq):
        sign = 1 if core == 0 else -1
        return [
            self.cycle[(self.place[seq] - sign * offset) % self.seqs] for offset in self.offsets
        ]

    def rank(self, core, seq):
        bits = self.seqs.bit_length() - 1
        if core == 1:
            return seq
        return int("".join(reversed(format(seq, f"0{bits}b"))), 2)

    def seq_of_rank(self, core, rank):
        return next(s for s in range(self.seqs) if self.rank(core, s) == rank)

    def across_rank(self, value, flip):
        def target(z, core, seq):
            return z * 2 + core, self.seq_of_rank(core, self.rank(core, seq) ^ flip)

        return self.permute(value, target)


def local_kernel(steps, a_ref, c_ref, down_ref, up_ref, low_f_ref, low_b_ref, grad_ref, acc_ref):
    step = pl.program_id(0)
    width = a_ref.shape[1]

    @pl.when(step == 0)
    def _():
        low_b_ref[...] = dot(c_ref[...], up_ref[...], ((1,), (1,))).astype(bf16)
        acc_ref[...] = jnp.zeros_like(acc_ref)

    block = a_ref[...]
    acc_ref[...] += dot(block, down_ref[...], ((1,), (1,)))
    grad_ref[step, :, :width] = dot(low_b_ref[...], block, ((0,), (0,)))

    @pl.when(step == steps - 1)
    def _():
        low_f = acc_ref[...].astype(bf16)
        low_f_ref[...] = low_f
        part = c_ref.shape[1] // steps
        for q in range(steps):
            grad_ref[q, :, width:] = dot(
                low_f, c_ref[:, q * part : (q + 1) * part], ((0,), (0,))
            )


def local_terms(a, c, down, up, steps):
    tokens, width = a.shape
    rank, keys = up.shape
    part = width // steps
    return pl.pallas_call(
        functools.partial(local_kernel, steps),
        grid=(steps,),
        in_specs=[
            pl.BlockSpec((tokens, part), lambda i: (0, i)),
            pl.BlockSpec((tokens, keys), lambda i: (0, 0)),
            pl.BlockSpec((rank, part), lambda i: (0, i)),
            pl.BlockSpec((rank, keys), lambda i: (0, 0)),
        ],
        out_specs=[
            pl.BlockSpec((tokens, rank), lambda i: (0, 0)),
            pl.BlockSpec((tokens, rank), lambda i: (0, 0)),
            pl.BlockSpec((steps, rank, part + keys // steps), lambda i: (0, 0, 0)),
        ],
        out_shape=[
            jax.ShapeDtypeStruct((tokens, rank), bf16),
            jax.ShapeDtypeStruct((tokens, rank), bf16),
            jax.ShapeDtypeStruct((steps, rank, part + keys // steps), f32),
        ],
        scratch_shapes=[pltpu.VMEM((tokens, rank), f32)],
        cost_estimate=pl.CostEstimate(
            flops=2 * tokens * width * 512, bytes_accessed=2 * tokens * width, transcendentals=0
        ),
        name="local_terms",
    )(a, c, down, up)


def slab_kernel(count, chunks, first, last, where_ref, *refs):
    refs = list(refs)
    pieces = [refs[:count], refs[count : 2 * count]]
    refs = refs[2 * count :]
    a_ref, c_ref, low_b_ref, down_ref = refs[:4]
    refs = refs[4:]
    if first:
        low_f_ref, up_ref = refs[:2]
        refs = refs[2:]
    else:
        acc_in_ref = refs[0]
        refs = refs[2:]
    keys_ref, grad_ref = refs[:2]
    acc_ref = refs[2] if last else keys_ref
    step = pl.program_id(0)
    part = c_ref.shape[1] // count

    @pl.when(step == 0)
    def _():
        if first:
            for j in range(count):
                at = pl.multiple_of(where_ref[2 + j] * part, part)
                acc_ref[:, j * part : (j + 1) * part] = adapter_scale * dot(
                    low_f_ref[...], up_ref[:, pl.ds(at, part)], ((1,), (0,))
                )
        else:
            acc_ref[...] = acc_in_ref[...]

    cot = jnp.concatenate(
        [
            c_ref[:, pl.ds(pl.multiple_of(where_ref[2 + j] * part, part), part)]
            for j in range(count)
        ],
        axis=1,
    )

    def work(held):
        panel = jnp.concatenate([ref[...] for ref in held], axis=1)
        acc_ref[...] += dot(a_ref[...], panel, ((1,), (0,)))
        grad = dot(cot, panel, ((1,), (1,)))
        grad += adapter_scale * dot(low_b_ref[...], down_ref[...], ((1,), (0,)))
        grad_ref[...] = grad.astype(bf16)

    for core in range(2):

        @pl.when(step // chunks == core)
        def _(core=core):
            work(pieces[core])

    if last:

        @pl.when(step == 2 * chunks - 1)
        def _():
            for j in range(count):
                at = pl.multiple_of(where_ref[2 + j] * part, part)
                keys_ref[:, pl.ds(at, part)] = acc_ref[:, j * part : (j + 1) * part].astype(bf16)


def slab(where, mine, other, a, c, low_b, down, low_f, up, acc, grad, first, last):
    count = len(mine)
    tokens, width = a.shape
    rank, keys = up.shape
    rows, part = mine[0].shape
    chunks = max(1, rows // 512)
    size = rows // chunks

    def row_block(i, where):
        return where[i // chunks] * chunks + i % chunks

    fixed = lambda i, where: (0, 0)
    in_specs = [
        pl.BlockSpec((size, part), lambda i, where: (jnp.minimum(i, chunks - 1), 0))
        for _ in range(count)
    ]
    in_specs += [
        pl.BlockSpec((size, part), lambda i, where: (jnp.maximum(i - chunks, 0), 0))
        for _ in range(count)
    ]
    in_specs += [
        pl.BlockSpec((tokens, size), lambda i, where: (0, row_block(i, where))),
        pl.BlockSpec((tokens, keys), fixed),
        pl.BlockSpec((tokens, rank), fixed),
        pl.BlockSpec((rank, size), lambda i, where: (0, row_block(i, where))),
    ]
    operands = [where, *mine, *other, a, c, low_b, down]
    aliases = {}
    if first:
        in_specs += [pl.BlockSpec((tokens, rank), fixed), pl.BlockSpec((rank, keys), fixed)]
        operands += [low_f, up]
    else:
        in_specs += [pl.BlockSpec((tokens, keys), fixed), pl.BlockSpec(memory_space=pl.ANY)]
        operands += [acc, grad]
        aliases = {len(operands) - 1: 1}
    return pl.pallas_call(
        functools.partial(slab_kernel, count, chunks, first, last),
        grid_spec=pltpu.PrefetchScalarGridSpec(
            num_scalar_prefetch=1,
            grid=(2 * chunks,),
            in_specs=in_specs,
            out_specs=[
                pl.BlockSpec((tokens, keys), fixed),
                pl.BlockSpec((tokens, size), lambda i, where: (0, row_block(i, where))),
            ],
            scratch_shapes=[pltpu.VMEM((tokens, keys), f32)] if last else [],
        ),
        out_shape=[
            jax.ShapeDtypeStruct((tokens, keys), bf16 if last else f32),
            jax.ShapeDtypeStruct((tokens, width), bf16),
        ],
        input_output_aliases=aliases,
        cost_estimate=pl.CostEstimate(
            flops=8 * tokens * rows * keys, bytes_accessed=16 * tokens * rows, transcendentals=0
        ),
        name="slab",
    )(*operands)


def reduce_over_seq(layout, partial, rank):
    half = partial.shape[0] // 2
    held = partial
    while half:
        bit = (rank // half) % 2
        kept = lax.dynamic_slice_in_dim(held, bit * half, half, 0)
        sent = lax.dynamic_slice_in_dim(held, (1 - bit) * half, half, 0)
        held = kept + layout.across_rank(sent, half)
        half //= 2
    half = 1
    while half < partial.shape[0]:
        bit = (rank // half) % 2
        other = layout.across_rank(held, half)
        both = jnp.concatenate([held, other], 0)
        swapped = jnp.concatenate([other, held], 0)
        held = jnp.where(bit == 0, both, swapped)
        half *= 2
    return held


def body(layout, activations, base_weight, adapter_down, adapter_up, cotangent):
    a, down, up, c = activations[0], adapter_down[0], adapter_up[0], cotangent[0]
    count = layout.seqs
    token_count = a.shape[0] * count
    blk, seq = lax.axis_index("blk"), lax.axis_index("seq")
    z, core = blk // 2, blk % 2
    columns = np.array(
        [[layout.column_of(k, s) for s in range(count)] for k in range(2)], np.int32
    )
    my_columns = jnp.asarray(columns)[core, seq]
    ranks = np.array([[layout.rank(k, s) for s in range(count)] for k in range(2)], np.int32)
    my_rank = jnp.asarray(ranks)[core, seq]
    where_of = []

    shifts = [0]
    for step in range(1, layout.depth // 2 + 1):
        shifts.append(step)
        if layout.depth - step != step:
            shifts.append(layout.depth - step)
    shards = {0: base_weight}
    for shift in shifts[1:]:
        shards[shift] = layout.along_depth(base_weight, shift)

    low_f, low_b, partial = local_terms(a, c, down, up, count)

    acc = grad = None
    for at, shift in enumerate(shifts):
        shard = shards[shift]
        forward, backward = [shard], [shard]
        for step in range(max(layout.forward_steps, layout.backward_steps)):
            if step < layout.forward_steps:
                forward.append(layout.along_cycle(forward[-1], 1))
            if step < layout.backward_steps:
                backward.append(layout.along_cycle(backward[-1], -1))
        mine = forward + backward[1:]
        swapped = [layout.swap_cores(piece) for piece in mine]
        by_offset = {-offset % count: piece for offset, piece in zip(layout.offsets, swapped)}
        other = [by_offset[offset % count] for offset in layout.offsets]
        source = (z - shift) % layout.depth
        where = jnp.concatenate(
            [jnp.stack([source * 2 + core, source * 2 + 1 - core]).astype(jnp.int32), my_columns]
        )
        acc, grad = slab(
            where, mine, other, a, c, low_b, down, low_f, up, acc, grad,
            at == 0, at == len(shifts) - 1,
        )

    sums = reduce_over_seq(layout, partial, my_rank) * (adapter_scale / token_count)
    width = a.shape[1] // count
    down_gradient = sums[:, :, :width].transpose(1, 0, 2).reshape(down.shape)
    up_gradient = sums[:, :, width:].transpose(1, 0, 2).reshape(up.shape)
    return acc[None], grad[None], down_gradient[None], up_gradient[None]


def solution(mesh):
    return jax.shard_map(
        functools.partial(body, Layout(mesh)),
        mesh=mesh,
        in_specs=(
            P("blk", "seq", None),
            P("blk", "seq"),
            P("blk", None, None),
            P("blk", None, None),
            P("blk", "seq", None),
        ),
        out_specs=(
            P("blk", "seq", None),
            P("blk", "seq", None),
            P("blk", None, None),
            P("blk", None, None),
        ),
        check_vma=False,
    )
```

```python
import functools

import jax
import jax.numpy as jnp
from jax import lax
from jax.experimental import pallas as pl
from jax.experimental.pallas import tpu as pltpu
from jax.sharding import PartitionSpec as P

adapter_scale = 2.0
axes = ("blk", "seq")
f32 = jnp.float32
bf16 = jnp.bfloat16


def dot(a, b, contract):
    return lax.dot_general(a, b, (contract, ((), ())), preferred_element_type=f32)


class Layout:
    def __init__(self, mesh):
        self.blocks, self.seqs = mesh.shape["blk"], mesh.shape["seq"]
        self.depth = self.blocks // 2
        self.cycle = list(range(0, self.seqs, 2)) + list(range(self.seqs - 1, 0, -2))
        self.place = {seq: at for at, seq in enumerate(self.cycle)}
        self.forward_steps = self.seqs // 2
        self.backward_steps = self.seqs - 1 - self.forward_steps
        self.offsets = [0] + list(range(1, self.forward_steps + 1))
        self.offsets += [-step for step in range(1, self.backward_steps + 1)]

    def permute(self, value, target):
        pairs = []
        for blk in range(self.blocks):
            for seq in range(self.seqs):
                to_blk, to_seq = target(blk // 2, blk % 2, seq)
                pairs.append((blk * self.seqs + seq, to_blk * self.seqs + to_seq))
        moved = lax.ppermute(value, axes, pairs)
        if value.dtype == bf16:
            moved = pltpu.with_memory_space_constraint(moved, pltpu.HBM)
        return moved

    def along_depth(self, value, shift):
        return self.permute(
            value, lambda z, core, seq: (((z + shift) % self.depth) * 2 + core, seq)
        )

    def along_cycle(self, value, step):
        def target(z, core, seq):
            sign = step if core == 0 else -step
            return z * 2 + core, self.cycle[(self.place[seq] + sign) % self.seqs]

        return self.permute(value, target)

    def swap_cores(self, value):
        return self.permute(value, lambda z, core, seq: (z * 2 + 1 - core, seq))

    def column_of(self, core, seq):
        sign = 1 if core == 0 else -1
        return [
            self.cycle[(self.place[seq] - sign * offset) % self.seqs] for offset in self.offsets
        ]

    def rank(self, core, seq):
        bits = self.seqs.bit_length() - 1
        if core == 1:
            return seq
        return int("".join(reversed(format(seq, f"0{bits}b"))), 2)

    def seq_of_rank(self, core, rank):
        return next(s for s in range(self.seqs) if self.rank(core, s) == rank)

    def across_rank(self, value, flip):
        def target(z, core, seq):
            return z * 2 + core, self.seq_of_rank(core, self.rank(core, seq) ^ flip)

        return self.permute(value, target)


def local_kernel(steps, a_ref, c_ref, down_ref, up_ref, low_f_ref, low_b_ref, grad_ref, acc_ref):
    step = pl.program_id(0)
    width = a_ref.shape[1]

    @pl.when(step == 0)
    def _():
        low_b_ref[...] = dot(c_ref[...], up_ref[...], ((1,), (1,))).astype(bf16)
        acc_ref[...] = jnp.zeros_like(acc_ref)

    block = a_ref[...]
    acc_ref[...] += dot(block, down_ref[...], ((1,), (1,)))
    here = pl.ds(pl.multiple_of(step * width, width), width)
    grad_ref[:, here] = dot(low_b_ref[...], block, ((0,), (0,)))

    @pl.when(step == steps - 1)
    def _():
        low_f = acc_ref[...].astype(bf16)
        low_f_ref[...] = low_f
        grad_ref[:, steps * width :] = dot(low_f, c_ref[...], ((0,), (0,)))


def local_terms(a, c, down, up, steps):
    tokens, width = a.shape
    rank, keys = up.shape
    part = width // steps
    return pl.pallas_call(
        functools.partial(local_kernel, steps),
        grid=(steps,),
        in_specs=[
            pl.BlockSpec((tokens, part), lambda i: (0, i)),
            pl.BlockSpec((tokens, keys), lambda i: (0, 0)),
            pl.BlockSpec((rank, part), lambda i: (0, i)),
            pl.BlockSpec((rank, keys), lambda i: (0, 0)),
        ],
        out_specs=[
            pl.BlockSpec((tokens, rank), lambda i: (0, 0)),
            pl.BlockSpec((tokens, rank), lambda i: (0, 0)),
            pl.BlockSpec((rank, width + keys), lambda i: (0, 0)),
        ],
        out_shape=[
            jax.ShapeDtypeStruct((tokens, rank), bf16),
            jax.ShapeDtypeStruct((tokens, rank), bf16),
            jax.ShapeDtypeStruct((rank, width + keys), f32),
        ],
        scratch_shapes=[pltpu.VMEM((tokens, rank), f32)],
        compiler_params=pltpu.CompilerParams(vmem_limit_bytes=16 << 20),
        cost_estimate=pl.CostEstimate(
            flops=1, bytes_accessed=1, transcendentals=0
        ),
        name="local_terms",
    )(a, c, down, up)


def slab_kernel(layout, shift, first, last, *refs):
    count = layout.seqs
    pieces = [refs[:count], refs[count : 2 * count]]
    a_ref, c_ref, low_b_ref, down_ref, *refs = refs[2 * count :]
    if first:
        low_f_ref, up_ref, *refs = refs
    else:
        acc_in_ref, _, *refs = refs
    keys_ref, grad_ref, panel_ref, rows_a_ref, cot_ref, rows_down_ref, out_ref, *refs = refs
    if last:
        acc_ref, *refs = refs
    else:
        acc_ref = keys_ref
    panel_sem, a_sem, cot_sem, down_sem, out_sem = refs
    rows, part = pieces[0][0].shape
    chunks, size = panel_sem.shape[1], out_ref.shape[2]

    blk, seq = lax.axis_index("blk"), lax.axis_index("seq")
    z, core = blk // 2, blk % 2
    source = lax.rem(z + (layout.depth - shift), layout.depth)
    starts = [
        pl.multiple_of((source * 2 + core) * rows, rows),
        pl.multiple_of((source * 2 + 1 - core) * rows, rows),
    ]
    columns = []
    for j in range(count):
        column = jnp.int32(0)
        for k in range(2):
            for s in range(count):
                here = jnp.logical_and(core == k, seq == s)
                column = jnp.where(here, layout.column_of(k, s)[j], column)
        columns.append(pl.ds(pl.multiple_of(column * part, part), part))
    places = [pl.ds(j * part, part) for j in range(count)]

    def cot_copy(j):
        return pltpu.make_async_copy(
            c_ref.at[:, columns[j]], cot_ref.at[:, places[j]], cot_sem.at[j]
        )

    def panel_copy(k, r, j):
        span = pl.ds(r * size, size)
        return pltpu.make_async_copy(
            pieces[k][j].at[span, :], panel_ref.at[k, span, places[j]], panel_sem.at[k, r, j]
        )

    def a_copy(k):
        return pltpu.make_async_copy(
            a_ref.at[:, pl.ds(starts[k], rows)], rows_a_ref.at[k], a_sem.at[k]
        )

    def down_copy(k):
        return pltpu.make_async_copy(
            down_ref.at[:, pl.ds(starts[k], rows)], rows_down_ref.at[k], down_sem.at[k]
        )

    def out_copy(k, r):
        to = pl.ds(pl.multiple_of(starts[k] + r * size, size), size)
        return pltpu.make_async_copy(
            out_ref.at[k * chunks + r], grad_ref.at[:, to], out_sem.at[k, r]
        )

    for j in range(count):
        cot_copy(j).start()
    for k in range(2):
        down_copy(k).start()
        for r in range(chunks):
            for j in range(count):
                panel_copy(k, r, j).start()
        a_copy(k).start()

    low_b = low_b_ref[...] * jnp.asarray(adapter_scale, bf16)
    if first:
        low_f = low_f_ref[...] * jnp.asarray(adapter_scale, bf16)
        for j in range(count):
            acc_ref[:, places[j]] = dot(low_f, up_ref[:, columns[j]], ((1,), (0,)))
    for j in range(count):
        cot_copy(j).wait()
    for k in range(2):
        down_copy(k).wait()
        for r in range(chunks):
            for j in range(count):
                panel_copy(k, r, j).wait()
            span = slice(r * size, (r + 1) * size)
            grad = dot(cot_ref[...], panel_ref[k, span, :], ((1,), (1,)))
            grad += dot(low_b, rows_down_ref[k, :, span], ((1,), (0,)))
            out_ref[k * chunks + r] = grad.astype(bf16)
            out_copy(k, r).start()
        a_copy(k).wait()
        base = acc_ref if first or k else acc_in_ref
        acc_ref[...] = base[...] + dot(rows_a_ref[k], panel_ref[k], ((1,), (0,)))
    if last:
        for j in range(count):
            keys_ref[:, columns[j]] = acc_ref[:, places[j]].astype(bf16)
    for k in range(2):
        for r in range(chunks):
            out_copy(k, r).wait()


def slab(layout, shift, mine, other, a, c, low_b, down, low_f, up, acc, grad, first, last):
    count = len(mine)
    tokens, width = a.shape
    rank, keys = up.shape
    rows = mine[0].shape[0]
    chunks = max(1, rows // 512)
    size = rows // chunks
    whole = pl.BlockSpec(memory_space=pltpu.VMEM)
    remote = pl.BlockSpec(memory_space=pl.ANY)
    held = [pltpu.with_memory_space_constraint(piece, pltpu.HBM) for piece in [*mine, *other]]
    in_specs = [remote] * (2 * count + 2) + [whole, remote]
    operands = [*held, a, c, low_b, down]
    aliases = {}
    if first:
        in_specs += [whole, whole]
        operands += [low_f, up]
    else:
        in_specs += [whole, remote]
        operands += [pltpu.with_memory_space_constraint(acc, pltpu.VMEM), grad]
        aliases = {len(operands) - 1: 1}
        if not last:
            aliases[len(operands) - 2] = 0
    keys_type = jax.ShapeDtypeStruct if last else pltpu.VMEM
    scratch = [
        pltpu.VMEM((2, rows, keys), bf16),
        pltpu.VMEM((2, tokens, rows), bf16),
        pltpu.VMEM((tokens, keys), bf16),
        pltpu.VMEM((2, rank, rows), bf16),
        pltpu.VMEM((2 * chunks, tokens, size), bf16),
    ]
    scratch += [pltpu.VMEM((tokens, keys), f32)] if last else []
    scratch += [
        pltpu.SemaphoreType.DMA((2, chunks, count)),
        pltpu.SemaphoreType.DMA((2,)),
        pltpu.SemaphoreType.DMA((count,)),
        pltpu.SemaphoreType.DMA((2,)),
        pltpu.SemaphoreType.DMA((2, chunks)),
    ]
    return pl.pallas_call(
        functools.partial(slab_kernel, layout, shift, first, last),
        in_specs=in_specs,
        out_specs=[whole, remote],
        scratch_shapes=scratch,
        out_shape=[
            keys_type((tokens, keys), bf16 if last else f32),
            jax.ShapeDtypeStruct((tokens, width), bf16),
        ],
        input_output_aliases=aliases,
        compiler_params=pltpu.CompilerParams(vmem_limit_bytes=24 << 20),
        cost_estimate=pl.CostEstimate(
            flops=1, bytes_accessed=1, transcendentals=0
        ),
        name="slab",
    )(*operands)


def stages_of(layout):
    depth, rounds = layout.depth, layout.forward_steps
    if (depth, layout.seqs) == (4, 4):
        exchanges = [
            ("turn", 0, 1),
            ("turn", 0, -1),
            ("turn", 0, 2),
            ("sum",),
            ("turn", 1, 1),
            ("turn", 1, -1),
            ("turn", 1, 2),
            ("turn", 2, 1),
            ("turn", 3, 1),
            ("turn", 2, 2),
            ("turn", 3, 2),
            ("sum",),
        ]
        besides = {
            0: [("rise", 1, 0, 0), ("local",)],
            2: [("rise", 2, 0, 0)],
            4: [("rise", 3, 0, 1)],
            5: [("slab", 0)],
            6: [("rise", 2, -1, 0)],
            8: [("rise", 3, -1, 1), ("slab", 1)],
            10: [("slab", 2)],
        }
        stages = []
        for at, exchange in enumerate(exchanges[:-1]):
            starts = exchanges[: 2] if at == 0 else exchanges[at + 1 : at + 2]
            starts = starts + besides.get(at, [])
            dones = [exchange]
            dones += [name for name in besides.get(at - 1, []) if name[0] == "rise"]
            stages.append((starts, dones))
        return stages
    stages = [([("local",), ("rise", 1, 0, 0)], [("rise", 1, 0, 0)])]
    for at in range(depth):
        for step in range(1, rounds + 1):
            starts = [("turn", at, step)]
            if step <= layout.backward_steps:
                starts.append(("turn", at, -step))
            dones = list(starts)
            if step == 1 and 0 < at < depth - 1:
                starts.append(("rise", at + 1, 0, 0))
            if step == rounds and at:
                dones.append(("rise", at + 1, 0, 0))
                starts.append(("slab", at - 1))
            stages.append((starts, dones))
    stages += [([("sum",)], [("sum",)])] * (layout.seqs.bit_length() - 1)
    return stages


def body(layout, activations, base_weight, adapter_down, adapter_up, cotangent):
    a, down, up, c = activations[0], adapter_down[0], adapter_up[0], cotangent[0]
    count, depth, width = layout.seqs, layout.depth, activations.shape[2]
    a, c, down, up = (pltpu.with_memory_space_constraint(x, pltpu.HBM) for x in (a, c, down, up))
    scale = adapter_scale / (a.shape[0] * count)

    shifts = [0]
    for step in range(1, depth // 2 + 1):
        shifts += [step] if 2 * step == depth else [step, depth - step]

    here = {("mine", 0, 0): base_weight}
    flying = {}
    state = {}
    flips = [layout.seqs >> step for step in range(1, layout.seqs.bit_length())]
    swapped = set()

    def result_of(name):
        return ("mine", *name[1:3]) if name[0] in ("turn", "rise") else name

    def multiply(at):
        for name in [name for name in flying if name[0] == "other" and name[1] == at]:
            here[name] = flying.pop(name)
        mine = [here[("mine", at, offset)] for offset in layout.offsets]
        other = [here.pop(("other", at, offset)) for offset in layout.offsets]
        state["acc"], state["grad"] = slab(
            layout, shifts[at], mine, other, a, c, state["low_b"], down, state["low_f"], up,
            state.get("acc"), state.get("grad"), at == 0, at == depth - 1,
        )

    def swap_ready():
        names = []
        for side, at, offset in list(here):
            turned = next(o for o in layout.offsets if (o + offset) % count == 0)
            name = ("other", at, turned)
            if side == "mine" and name not in swapped:
                swapped.add(name)
                flying[name] = layout.swap_cores(here[(side, at, offset)])
                names.append(name)
        return names

    def start(name):
        if name[0] == "local":
            state["low_f"], state["low_b"], state["sum"] = local_terms(a, c, down, up, count)
        elif name[0] == "slab":
            multiply(name[1])
        elif name[0] == "rise":
            _, at, offset, source = name
            shift = (shifts[at] - shifts[source]) % depth
            flying[result_of(name)] = layout.along_depth(here[("mine", source, offset)], shift)
        elif name[0] == "sum":
            flying[name] = layout.across_rank(state["sum"], flips.pop(0))
        else:
            _, at, offset = name
            step = 1 if offset > 0 else -1
            flying[result_of(name)] = layout.along_cycle(here[("mine", at, offset - step)], step)

    def close(names):
        for name in names:
            if name in flying:
                value = flying.pop(name)
                if name[0] == "sum":
                    state["sum"] = state["sum"] + value
                else:
                    here[name] = value
        new_here, new_state = lax.optimization_barrier((dict(here), dict(state)))
        here.update(new_here)
        state.update(new_state)

    turning = []
    for starts, dones in stages_of(layout):
        for name in starts:
            if name[0] not in ("local", "slab"):
                start(name)
        late, turning = turning, swap_ready()
        for name in starts:
            if name[0] in ("local", "slab"):
                start(name)
        close([result_of(name) for name in dones] + late)
    close([name for name in flying if name[0] != "sum"])
    swap_ready()
    multiply(depth - 1)
    sums = state["sum"]
    if "sum" in [name[0] for name in flying]:
        sums = sums + flying[("sum",)]
    state["down"], state["up"] = sums[:, :width] * scale, sums[:, width:] * scale
    return tuple(state[name][None] for name in ("acc", "grad", "down", "up"))


def solution(mesh):
    return jax.shard_map(
        functools.partial(body, Layout(mesh)),
        mesh=mesh,
        in_specs=(
            P("blk", "seq", None),
            P("blk", "seq"),
            P("blk", None, None),
            P("blk", None, None),
            P("blk", "seq", None),
        ),
        out_specs=(
            P("blk", "seq", None),
            P("blk", "seq", None),
            P("blk", None, None),
            P("blk", None, None),
        ),
        check_vma=False,
    )
```

```python
import functools

import jax
import jax.numpy as jnp
from jax import lax
from jax.experimental import pallas as pl
from jax.experimental.pallas import tpu as pltpu
from jax.sharding import PartitionSpec as P

adapter_scale = 2.0
axes = ("blk", "seq")
f32 = jnp.float32
bf16 = jnp.bfloat16


def dot(a, b, contract):
    return lax.dot_general(a, b, (contract, ((), ())), preferred_element_type=f32)


class Layout:
    def __init__(self, mesh):
        self.blocks, self.seqs = mesh.shape["blk"], mesh.shape["seq"]
        self.depth = self.blocks // 2
        self.cycle = list(range(0, self.seqs, 2)) + list(range(self.seqs - 1, 0, -2))
        self.place = {seq: at for at, seq in enumerate(self.cycle)}
        self.forward_steps = self.seqs // 2
        self.backward_steps = self.seqs - 1 - self.forward_steps
        self.offsets = [0] + list(range(1, self.forward_steps + 1))
        self.offsets += [-step for step in range(1, self.backward_steps + 1)]

    def permute(self, value, target):
        pairs = []
        for blk in range(self.blocks):
            for seq in range(self.seqs):
                to_blk, to_seq = target(blk // 2, blk % 2, seq)
                pairs.append((blk * self.seqs + seq, to_blk * self.seqs + to_seq))
        moved = lax.ppermute(value, axes, pairs)
        if value.dtype == bf16:
            moved = pltpu.with_memory_space_constraint(moved, pltpu.HBM)
        return moved

    def along_depth(self, value, shift):
        return self.permute(
            value, lambda z, core, seq: (((z + shift) % self.depth) * 2 + core, seq)
        )

    def along_cycle(self, value, step):
        def target(z, core, seq):
            sign = step if core == 0 else -step
            return z * 2 + core, self.cycle[(self.place[seq] + sign) % self.seqs]

        return self.permute(value, target)

    def swap_cores(self, value):
        return self.permute(value, lambda z, core, seq: (z * 2 + 1 - core, seq))

    def column_of(self, core, seq):
        sign = 1 if core == 0 else -1
        return [
            self.cycle[(self.place[seq] - sign * offset) % self.seqs] for offset in self.offsets
        ]

    def rank(self, core, seq):
        bits = self.seqs.bit_length() - 1
        if core == 1:
            return seq
        return int("".join(reversed(format(seq, f"0{bits}b"))), 2)

    def seq_of_rank(self, core, rank):
        return next(s for s in range(self.seqs) if self.rank(core, s) == rank)

    def across_rank(self, value, flip):
        def target(z, core, seq):
            return z * 2 + core, self.seq_of_rank(core, self.rank(core, seq) ^ flip)

        return self.permute(value, target)


def local_kernel(steps, a_ref, c_ref, down_ref, up_ref, low_f_ref, low_b_ref, grad_ref, acc_ref):
    step = pl.program_id(0)
    width = a_ref.shape[1]

    @pl.when(step == 0)
    def _():
        low_b_ref[...] = dot(c_ref[...], up_ref[...], ((1,), (1,))).astype(bf16)
        acc_ref[...] = jnp.zeros_like(acc_ref)

    block = a_ref[...]
    acc_ref[...] += dot(block, down_ref[...], ((1,), (1,)))
    here = pl.ds(pl.multiple_of(step * width, width), width)
    grad_ref[:, here] = dot(low_b_ref[...], block, ((0,), (0,)))

    @pl.when(step == steps - 1)
    def _():
        low_f = acc_ref[...].astype(bf16)
        low_f_ref[...] = low_f
        grad_ref[:, steps * width :] = dot(low_f, c_ref[...], ((0,), (0,)))


def local_terms(a, c, down, up, steps):
    tokens, width = a.shape
    rank, keys = up.shape
    part = width // steps
    return pl.pallas_call(
        functools.partial(local_kernel, steps),
        grid=(steps,),
        in_specs=[
            pl.BlockSpec((tokens, part), lambda i: (0, i)),
            pl.BlockSpec((tokens, keys), lambda i: (0, 0)),
            pl.BlockSpec((rank, part), lambda i: (0, i)),
            pl.BlockSpec((rank, keys), lambda i: (0, 0)),
        ],
        out_specs=[
            pl.BlockSpec((tokens, rank), lambda i: (0, 0)),
            pl.BlockSpec((tokens, rank), lambda i: (0, 0)),
            pl.BlockSpec((rank, width + keys), lambda i: (0, 0)),
        ],
        out_shape=[
            jax.ShapeDtypeStruct((tokens, rank), bf16),
            jax.ShapeDtypeStruct((tokens, rank), bf16),
            jax.ShapeDtypeStruct((rank, width + keys), f32),
        ],
        scratch_shapes=[pltpu.VMEM((tokens, rank), f32)],
        compiler_params=pltpu.CompilerParams(vmem_limit_bytes=16 << 20),
        cost_estimate=pl.CostEstimate(
            flops=1, bytes_accessed=1, transcendentals=0
        ),
        name="local_terms",
    )(a, c, down, up)


def slab_kernel(layout, shift, first, last, *refs):
    count = layout.seqs
    pieces = [refs[:count], refs[count : 2 * count]]
    a_ref, c_ref, low_b_ref, down_ref, *refs = refs[2 * count :]
    if first:
        low_f_ref, up_ref, *refs = refs
    else:
        acc_in_ref, _, *refs = refs
    keys_ref, grad_ref, panel_ref, rows_a_ref, cot_ref, rows_down_ref, out_ref, *refs = refs
    if last:
        acc_ref, keys_out_ref, keys_sem, *refs = refs
    else:
        acc_ref = keys_ref
    panel_sem, a_sem, cot_sem, down_sem, out_sem = refs
    rows, part = pieces[0][0].shape
    chunks, size = panel_sem.shape[1], out_ref.shape[2]

    blk, seq = lax.axis_index("blk"), lax.axis_index("seq")
    z, core = blk // 2, blk % 2
    source = lax.rem(z + (layout.depth - shift), layout.depth)
    starts = [
        pl.multiple_of((source * 2 + core) * rows, rows),
        pl.multiple_of((source * 2 + 1 - core) * rows, rows),
    ]
    columns = []
    for j in range(count):
        column = jnp.int32(0)
        for k in range(2):
            for s in range(count):
                here = jnp.logical_and(core == k, seq == s)
                column = jnp.where(here, layout.column_of(k, s)[j], column)
        columns.append(pl.ds(pl.multiple_of(column * part, part), part))
    places = [pl.ds(j * part, part) for j in range(count)]

    def cot_copy(j):
        return pltpu.make_async_copy(
            c_ref.at[:, columns[j]], cot_ref.at[:, places[j]], cot_sem.at[j]
        )

    def panel_copy(k, r, j):
        span = pl.ds(r * size, size)
        return pltpu.make_async_copy(
            pieces[k][j].at[span, :], panel_ref.at[k, span, places[j]], panel_sem.at[k, r, j]
        )

    def a_copy(k):
        return pltpu.make_async_copy(
            a_ref.at[:, pl.ds(starts[k], rows)], rows_a_ref.at[k], a_sem.at[k]
        )

    def down_copy(k):
        return pltpu.make_async_copy(
            down_ref.at[:, pl.ds(starts[k], rows)], rows_down_ref.at[k], down_sem.at[k]
        )

    def out_copy(k, r):
        to = pl.ds(pl.multiple_of(starts[k] + r * size, size), size)
        return pltpu.make_async_copy(
            out_ref.at[k * chunks + r], grad_ref.at[:, to], out_sem.at[k, r]
        )

    def keys_copy(j):
        return pltpu.make_async_copy(
            keys_out_ref.at[:, places[j]], keys_ref.at[:, columns[j]], keys_sem.at[j]
        )

    def fetch(k, r):
        for j in range(count):
            panel_copy(k, r, j).start()

    def landed(k, rs=range(chunks)):
        for r in rs:
            for j in range(count):
                panel_copy(k, r, j).wait()

    def frozen_gradient(k, r):
        span = slice(r * size, (r + 1) * size)
        grad = dot(cot_ref[...], panel_ref[k, span, :], ((1,), (1,)))
        grad += dot(low_b, rows_down_ref[k, :, span], ((1,), (0,)))
        out_ref[k * chunks + r] = grad.astype(bf16)
        out_copy(k, r).start()

    def add_keys(k):
        a_copy(k).wait()
        base = acc_ref if first or k else acc_in_ref
        acc_ref[...] = base[...] + dot(rows_a_ref[k], panel_ref[k], ((1,), (0,)))

    for j in range(count):
        cot_copy(j).start()
    for k in range(2):
        down_copy(k).start()
        for r in range(chunks):
            fetch(k, r)
        a_copy(k).start()
    low_b = low_b_ref[...] * jnp.asarray(adapter_scale, bf16)
    if first:
        low_f = low_f_ref[...] * jnp.asarray(adapter_scale, bf16)
        for j in range(count):
            acc_ref[:, places[j]] = dot(low_f, up_ref[:, columns[j]], ((1,), (0,)))
    for j in range(count):
        cot_copy(j).wait()
    for k in range(2):
        down_copy(k).wait()
    for r in range(chunks):
        landed(0, [r])
        frozen_gradient(0, r)
    add_keys(0)
    landed(1)
    if last:
        add_keys(1)
        for j in range(count):
            keys_out_ref[:, places[j]] = acc_ref[:, places[j]].astype(bf16)
            keys_copy(j).start()
    for r in range(chunks):
        frozen_gradient(1, r)
    if last:
        for j in range(count):
            keys_copy(j).wait()
    else:
        add_keys(1)
    for k in range(2):
        for r in range(chunks):
            out_copy(k, r).wait()


def slab(layout, shift, mine, other, a, c, low_b, down, low_f, up, acc, grad, first, last):
    count = len(mine)
    tokens, width = a.shape
    rank, keys = up.shape
    rows = mine[0].shape[0]
    chunks = max(1, rows // 512)
    size = rows // chunks
    whole = pl.BlockSpec(memory_space=pltpu.VMEM)
    remote = pl.BlockSpec(memory_space=pl.ANY)
    held = [pltpu.with_memory_space_constraint(piece, pltpu.HBM) for piece in [*mine, *other]]
    in_specs = [remote] * (2 * count + 2) + [whole, remote]
    operands = [*held, a, c, low_b, down]
    aliases = {}
    if first:
        in_specs += [whole, whole]
        operands += [low_f, up]
    else:
        in_specs += [whole, remote]
        operands += [pltpu.with_memory_space_constraint(acc, pltpu.VMEM), grad]
        aliases = {len(operands) - 1: 1}
        if not last:
            aliases[len(operands) - 2] = 0
    keys_type = jax.ShapeDtypeStruct if last else pltpu.VMEM
    scratch = [
        pltpu.VMEM((2, rows, keys), bf16),
        pltpu.VMEM((2, tokens, rows), bf16),
        pltpu.VMEM((tokens, keys), bf16),
        pltpu.VMEM((2, rank, rows), bf16),
        pltpu.VMEM((2 * chunks, tokens, size), bf16),
    ]
    if last:
        scratch += [
            pltpu.VMEM((tokens, keys), f32),
            pltpu.VMEM((tokens, keys), bf16),
            pltpu.SemaphoreType.DMA((count,)),
        ]
    scratch += [
        pltpu.SemaphoreType.DMA((2, chunks, count)),
        pltpu.SemaphoreType.DMA((2,)),
        pltpu.SemaphoreType.DMA((count,)),
        pltpu.SemaphoreType.DMA((2,)),
        pltpu.SemaphoreType.DMA((2, chunks)),
    ]
    return pl.pallas_call(
        functools.partial(slab_kernel, layout, shift, first, last),
        in_specs=in_specs,
        out_specs=[remote if last else whole, remote],
        scratch_shapes=scratch,
        out_shape=[
            keys_type((tokens, keys), bf16 if last else f32),
            jax.ShapeDtypeStruct((tokens, width), bf16),
        ],
        input_output_aliases=aliases,
        compiler_params=pltpu.CompilerParams(vmem_limit_bytes=24 << 20),
        cost_estimate=pl.CostEstimate(
            flops=1, bytes_accessed=1, transcendentals=0
        ),
        name="slab",
    )(*operands)


def stages_of(layout):
    depth, rounds = layout.depth, layout.forward_steps
    if (depth, layout.seqs) == (4, 4):
        exchanges = [
            ("turn", 0, 1),
            ("turn", 0, -1),
            ("turn", 0, 2),
            ("sum",),
            ("turn", 1, 1),
            ("turn", 1, -1),
            ("turn", 2, 1),
            ("turn", 1, 2),
            ("turn", 2, 2),
            ("turn", 3, 1),
            ("sum",),
            ("turn", 3, 2),
        ]
        besides = {
            0: [("rise", 1, 0, 0), ("local",)],
            2: [("rise", 2, 0, 0)],
            4: [("rise", 3, 0, 1), ("slab", 0)],
            6: [("rise", 2, -1, 0)],
            8: [("rise", 3, -1, 1), ("slab", 1)],
            10: [("slab", 2)],
        }
        stages = []
        for at, exchange in enumerate(exchanges):
            starts = exchanges[: 2] if at == 0 else exchanges[at + 1 : at + 2]
            starts = starts + besides.get(at, [])
            dones = [exchange]
            dones += [name for name in besides.get(at - 1, []) if name[0] == "rise"]
            stages.append((starts, dones))
        return stages
    stages = [([("local",), ("rise", 1, 0, 0)], [("rise", 1, 0, 0)])]
    for at in range(depth):
        for step in range(1, rounds + 1):
            starts = [("turn", at, step)]
            if step <= layout.backward_steps:
                starts.append(("turn", at, -step))
            dones = list(starts)
            if step == 1 and 0 < at < depth - 1:
                starts.append(("rise", at + 1, 0, 0))
            if step == rounds and at:
                dones.append(("rise", at + 1, 0, 0))
                starts.append(("slab", at - 1))
            stages.append((starts, dones))
    stages += [([("sum",)], [("sum",)])] * (layout.seqs.bit_length() - 1)
    return stages


def body(layout, activations, base_weight, adapter_down, adapter_up, cotangent):
    a, down, up, c = activations[0], adapter_down[0], adapter_up[0], cotangent[0]
    count, depth, width = layout.seqs, layout.depth, activations.shape[2]
    a, c, down, up = (pltpu.with_memory_space_constraint(x, pltpu.HBM) for x in (a, c, down, up))
    scale = adapter_scale / (a.shape[0] * count)

    shifts = [0]
    for step in range(1, depth // 2 + 1):
        shifts += [step] if 2 * step == depth else [step, depth - step]

    here = {("mine", 0, 0): base_weight}
    flying = {}
    state = {}
    flips = [layout.seqs >> step for step in range(1, layout.seqs.bit_length())]
    swapped = set()

    def result_of(name):
        return ("mine", *name[1:3]) if name[0] in ("turn", "rise") else name

    def multiply(at):
        swap_ready(at)
        for name in [name for name in flying if name[0] == "other" and name[1] == at]:
            here[name] = flying.pop(name)
        mine = [here[("mine", at, offset)] for offset in layout.offsets]
        other = [here.pop(("other", at, offset)) for offset in layout.offsets]
        state["acc"], state["grad"] = slab(
            layout, shifts[at], mine, other, a, c, state["low_b"], down, state["low_f"], up,
            state.get("acc"), state.get("grad"), at == 0, at == depth - 1,
        )

    def swap_ready(only=None, most=2):
        names = []
        for side, at, offset in list(here):
            turned = next(o for o in layout.offsets if (o + offset) % count == 0)
            name = ("other", at, turned)
            if side != "mine" or name in swapped or only not in (None, at):
                continue
            if only is None and len(names) == most:
                break
            swapped.add(name)
            flying[name] = layout.swap_cores(here[(side, at, offset)])
            names.append(name)
        return names

    def start(name):
        if name[0] == "local":
            state["low_f"], state["low_b"], state["sum"] = local_terms(a, c, down, up, count)
        elif name[0] == "slab":
            multiply(name[1])
        elif name[0] == "rise":
            _, at, offset, source = name
            shift = (shifts[at] - shifts[source]) % depth
            flying[result_of(name)] = layout.along_depth(here[("mine", source, offset)], shift)
        elif name[0] == "sum":
            flying[name] = layout.across_rank(state["sum"], flips.pop(0))
        else:
            _, at, offset = name
            step = 1 if offset > 0 else -1
            flying[result_of(name)] = layout.along_cycle(here[("mine", at, offset - step)], step)

    def close(names):
        for name in names:
            if name in flying:
                value = flying.pop(name)
                if name[0] == "sum":
                    state["sum"] = state["sum"] + value
                else:
                    here[name] = value
        new_here, new_state = lax.optimization_barrier((dict(here), dict(state)))
        here.update(new_here)
        state.update(new_state)

    for starts, dones in stages_of(layout):
        for name in starts:
            if name[0] not in ("local", "slab"):
                start(name)
        turning = swap_ready()
        for name in starts:
            if name[0] in ("local", "slab"):
                start(name)
        close([result_of(name) for name in dones] + turning)
    multiply(depth - 1)
    sums = state["sum"]
    state["down"], state["up"] = sums[:, :width] * scale, sums[:, width:] * scale
    return tuple(state[name][None] for name in ("acc", "grad", "down", "up"))


def solution(mesh):
    return jax.shard_map(
        functools.partial(body, Layout(mesh)),
        mesh=mesh,
        in_specs=(
            P("blk", "seq", None),
            P("blk", "seq"),
            P("blk", None, None),
            P("blk", None, None),
            P("blk", "seq", None),
        ),
        out_specs=(
            P("blk", "seq", None),
            P("blk", "seq", None),
            P("blk", None, None),
            P("blk", None, None),
        ),
        check_vma=False,
    )
```

```python
import functools

import jax
import jax.numpy as jnp
from jax import lax
from jax.experimental import pallas as pl
from jax.experimental.pallas import tpu as pltpu
from jax.sharding import PartitionSpec as P

adapter_scale = 2.0
axes = ("blk", "seq")
f32 = jnp.float32
bf16 = jnp.bfloat16


def dot(a, b, contract):
    return lax.dot_general(a, b, (contract, ((), ())), preferred_element_type=f32)


class Layout:
    def __init__(self, mesh):
        self.blocks, self.seqs = mesh.shape["blk"], mesh.shape["seq"]
        self.depth = self.blocks // 2
        self.cycle = list(range(0, self.seqs, 2)) + list(range(self.seqs - 1, 0, -2))
        self.place = {seq: at for at, seq in enumerate(self.cycle)}
        self.forward_steps = self.seqs // 2
        self.backward_steps = self.seqs - 1 - self.forward_steps
        self.offsets = [0] + list(range(1, self.forward_steps + 1))
        self.offsets += [-step for step in range(1, self.backward_steps + 1)]

    def permute(self, value, target):
        pairs = []
        for blk in range(self.blocks):
            for seq in range(self.seqs):
                to_blk, to_seq = target(blk // 2, blk % 2, seq)
                pairs.append((blk * self.seqs + seq, to_blk * self.seqs + to_seq))
        return lax.ppermute(value, axes, pairs)

    def along_depth(self, value, shift):
        return self.permute(
            value, lambda z, core, seq: (((z + shift) % self.depth) * 2 + core, seq)
        )

    def along_cycle(self, value, step):
        def target(z, core, seq):
            sign = step if core == 0 else -step
            return z * 2 + core, self.cycle[(self.place[seq] + sign) % self.seqs]

        return self.permute(value, target)

    def swap_cores(self, value):
        return self.permute(value, lambda z, core, seq: (z * 2 + 1 - core, seq))

    def column_of(self, core, seq):
        sign = 1 if core == 0 else -1
        return [
            self.cycle[(self.place[seq] - sign * offset) % self.seqs] for offset in self.offsets
        ]

    def rank(self, core, seq):
        bits = self.seqs.bit_length() - 1
        if core == 1:
            return seq
        return int("".join(reversed(format(seq, f"0{bits}b"))), 2)

    def seq_of_rank(self, core, rank):
        return next(s for s in range(self.seqs) if self.rank(core, s) == rank)

    def across_rank(self, value, flip):
        def target(z, core, seq):
            return z * 2 + core, self.seq_of_rank(core, self.rank(core, seq) ^ flip)

        return self.permute(value, target)


def local_kernel(steps, a_ref, c_ref, down_ref, up_ref, low_f_ref, low_b_ref, grad_ref, acc_ref):
    step = pl.program_id(0)
    width = a_ref.shape[1]

    @pl.when(step == 0)
    def _():
        low_b_ref[...] = dot(c_ref[...], up_ref[...], ((1,), (1,))).astype(bf16)
        acc_ref[...] = jnp.zeros_like(acc_ref)

    block = a_ref[...]
    acc_ref[...] += dot(block, down_ref[...], ((1,), (1,)))
    here = pl.ds(pl.multiple_of(step * width, width), width)
    grad_ref[:, here] = dot(low_b_ref[...], block, ((0,), (0,)))

    @pl.when(step == steps - 1)
    def _():
        low_f = acc_ref[...].astype(bf16)
        low_f_ref[...] = low_f
        grad_ref[:, steps * width :] = dot(low_f, c_ref[...], ((0,), (0,)))


def local_terms(a, c, down, up, steps):
    tokens, width = a.shape
    rank, keys = up.shape
    part = width // steps
    return pl.pallas_call(
        functools.partial(local_kernel, steps),
        grid=(steps,),
        in_specs=[
            pl.BlockSpec((tokens, part), lambda i: (0, i)),
            pl.BlockSpec((tokens, keys), lambda i: (0, 0)),
            pl.BlockSpec((rank, part), lambda i: (0, i)),
            pl.BlockSpec((rank, keys), lambda i: (0, 0)),
        ],
        out_specs=[
            pl.BlockSpec((tokens, rank), lambda i: (0, 0)),
            pl.BlockSpec((tokens, rank), lambda i: (0, 0)),
            pl.BlockSpec((rank, width + keys), lambda i: (0, 0)),
        ],
        out_shape=[
            jax.ShapeDtypeStruct((tokens, rank), bf16),
            jax.ShapeDtypeStruct((tokens, rank), bf16),
            jax.ShapeDtypeStruct((rank, width + keys), f32),
        ],
        scratch_shapes=[pltpu.VMEM((tokens, rank), f32)],
        compiler_params=pltpu.CompilerParams(vmem_limit_bytes=16 << 20),
        cost_estimate=pl.CostEstimate(
            flops=1, bytes_accessed=1, transcendentals=0
        ),
        name="local_terms",
    )(a, c, down, up)


def slab_kernel(layout, shift, first, last, *refs):
    count = layout.seqs
    pieces = [refs[:count], refs[count : 2 * count]]
    a_ref, c_ref, low_b_ref, down_ref, *refs = refs[2 * count :]
    if first:
        low_f_ref, up_ref, *refs = refs
    else:
        acc_in_ref, _, *refs = refs
    keys_ref, grad_ref, panel_ref, rows_a_ref, cot_ref, rows_down_ref, out_ref, *refs = refs
    if last:
        acc_ref, keys_out_ref, keys_sem, *refs = refs
    else:
        acc_ref = keys_ref
    panel_sem, a_sem, cot_sem, down_sem, out_sem = refs
    rows, part = pieces[0][0].shape
    chunks, size = panel_sem.shape[1], out_ref.shape[2]

    blk, seq = lax.axis_index("blk"), lax.axis_index("seq")
    z, core = blk // 2, blk % 2
    source = lax.rem(z + (layout.depth - shift), layout.depth)
    starts = [
        pl.multiple_of((source * 2 + core) * rows, rows),
        pl.multiple_of((source * 2 + 1 - core) * rows, rows),
    ]
    columns = []
    for j in range(count):
        column = jnp.int32(0)
        for k in range(2):
            for s in range(count):
                here = jnp.logical_and(core == k, seq == s)
                column = jnp.where(here, layout.column_of(k, s)[j], column)
        columns.append(pl.ds(pl.multiple_of(column * part, part), part))
    places = [pl.ds(j * part, part) for j in range(count)]

    def cot_copy(j):
        return pltpu.make_async_copy(
            c_ref.at[:, columns[j]], cot_ref.at[:, places[j]], cot_sem.at[j]
        )

    def panel_copy(k, r, j):
        span = pl.ds(r * size, size)
        return pltpu.make_async_copy(
            pieces[k][j].at[span, :], panel_ref.at[k, span, places[j]], panel_sem.at[k, r, j]
        )

    def a_copy(k):
        return pltpu.make_async_copy(
            a_ref.at[:, pl.ds(starts[k], rows)], rows_a_ref.at[k], a_sem.at[k]
        )

    def down_copy(k):
        return pltpu.make_async_copy(
            down_ref.at[:, pl.ds(starts[k], rows)], rows_down_ref.at[k], down_sem.at[k]
        )

    def out_copy(k, r):
        to = pl.ds(pl.multiple_of(starts[k] + r * size, size), size)
        return pltpu.make_async_copy(
            out_ref.at[k * chunks + r], grad_ref.at[:, to], out_sem.at[k, r]
        )

    def keys_copy(j):
        return pltpu.make_async_copy(
            keys_out_ref.at[:, places[j]], keys_ref.at[:, columns[j]], keys_sem.at[j]
        )

    def fetch(k, r):
        for j in range(count):
            panel_copy(k, r, j).start()

    def landed(k, rs=range(chunks)):
        for r in rs:
            for j in range(count):
                panel_copy(k, r, j).wait()

    def frozen_gradient(k, r):
        span = slice(r * size, (r + 1) * size)
        grad = dot(cot_ref[...], panel_ref[k, span, :], ((1,), (1,)))
        grad += dot(low_b, rows_down_ref[k, :, span], ((1,), (0,)))
        out_ref[k * chunks + r] = grad.astype(bf16)
        out_copy(k, r).start()

    def add_keys(k):
        a_copy(k).wait()
        base = acc_ref if first or k else acc_in_ref
        acc_ref[...] = base[...] + dot(rows_a_ref[k], panel_ref[k], ((1,), (0,)))

    for j in range(count):
        cot_copy(j).start()
    for k in range(2):
        down_copy(k).start()
        for r in range(chunks):
            fetch(k, r)
        a_copy(k).start()
    low_b = low_b_ref[...] * jnp.asarray(adapter_scale, bf16)
    if first:
        low_f = low_f_ref[...] * jnp.asarray(adapter_scale, bf16)
        for j in range(count):
            acc_ref[:, places[j]] = dot(low_f, up_ref[:, columns[j]], ((1,), (0,)))
    for j in range(count):
        cot_copy(j).wait()
    for k in range(2):
        down_copy(k).wait()
    for r in range(chunks):
        landed(0, [r])
        frozen_gradient(0, r)
    add_keys(0)
    landed(1)
    if last:
        add_keys(1)
        for j in range(count):
            keys_out_ref[:, places[j]] = acc_ref[:, places[j]].astype(bf16)
            keys_copy(j).start()
    for r in range(chunks):
        frozen_gradient(1, r)
    if last:
        for j in range(count):
            keys_copy(j).wait()
    else:
        add_keys(1)
    for k in range(2):
        for r in range(chunks):
            out_copy(k, r).wait()


def slab(layout, shift, mine, other, a, c, low_b, down, low_f, up, acc, grad, first, last):
    count = len(mine)
    tokens, width = a.shape
    rank, keys = up.shape
    rows = mine[0].shape[0]
    chunks = max(1, rows // 512)
    size = rows // chunks
    whole = pl.BlockSpec(memory_space=pltpu.VMEM)
    remote = pl.BlockSpec(memory_space=pl.ANY)
    in_specs = [remote] * (2 * count + 2) + [whole, remote]
    operands = [*mine, *other, a, c, low_b, down]
    aliases = {}
    if first:
        in_specs += [whole, whole]
        operands += [low_f, up]
    else:
        in_specs += [whole, remote]
        operands += [pltpu.with_memory_space_constraint(acc, pltpu.VMEM), grad]
        aliases = {len(operands) - 1: 1}
        if not last:
            aliases[len(operands) - 2] = 0
    keys_type = jax.ShapeDtypeStruct if last else pltpu.VMEM
    scratch = [
        pltpu.VMEM((2, rows, keys), bf16),
        pltpu.VMEM((2, tokens, rows), bf16),
        pltpu.VMEM((tokens, keys), bf16),
        pltpu.VMEM((2, rank, rows), bf16),
        pltpu.VMEM((2 * chunks, tokens, size), bf16),
    ]
    if last:
        scratch += [
            pltpu.VMEM((tokens, keys), f32),
            pltpu.VMEM((tokens, keys), bf16),
            pltpu.SemaphoreType.DMA((count,)),
        ]
    scratch += [
        pltpu.SemaphoreType.DMA((2, chunks, count)),
        pltpu.SemaphoreType.DMA((2,)),
        pltpu.SemaphoreType.DMA((count,)),
        pltpu.SemaphoreType.DMA((2,)),
        pltpu.SemaphoreType.DMA((2, chunks)),
    ]
    return pl.pallas_call(
        functools.partial(slab_kernel, layout, shift, first, last),
        in_specs=in_specs,
        out_specs=[remote if last else whole, remote],
        scratch_shapes=scratch,
        out_shape=[
            keys_type((tokens, keys), bf16 if last else f32),
            jax.ShapeDtypeStruct((tokens, width), bf16),
        ],
        input_output_aliases=aliases,
        compiler_params=pltpu.CompilerParams(vmem_limit_bytes=24 << 20),
        cost_estimate=pl.CostEstimate(
            flops=1, bytes_accessed=1, transcendentals=0
        ),
        name="slab",
    )(*operands)


def stages_of(layout):
    depth, rounds = layout.depth, layout.forward_steps
    if (depth, layout.seqs) == (4, 4):
        exchanges = [
            ("turn", 0, 1),
            ("turn", 0, -1),
            ("turn", 0, 2),
            ("sum",),
            ("turn", 1, 1),
            ("turn", 1, -1),
            ("turn", 2, 1),
            ("turn", 1, 2),
            ("turn", 2, 2),
            ("turn", 3, 1),
            ("sum",),
            ("turn", 3, 2),
        ]
        besides = {
            0: [("rise", 1, 0, 0), ("local",)],
            2: [("rise", 2, 0, 0)],
            4: [("rise", 3, 0, 1)],
            5: [("slab", 0)],
            6: [("rise", 2, -1, 0)],
            8: [("rise", 3, -1, 1)],
            9: [("slab", 1)],
            10: [("slab", 2)],
        }
        stages = []
        for at, exchange in enumerate(exchanges):
            starts = exchanges[: 2] if at == 0 else exchanges[at + 1 : at + 2]
            starts = starts + besides.get(at, [])
            dones = [exchange]
            dones += [name for name in besides.get(at - 1, []) if name[0] == "rise"]
            stages.append((starts, dones))
        return stages
    stages = [([("local",), ("rise", 1, 0, 0)], [("rise", 1, 0, 0)])]
    for at in range(depth):
        for step in range(1, rounds + 1):
            starts = [("turn", at, step)]
            if step <= layout.backward_steps:
                starts.append(("turn", at, -step))
            dones = list(starts)
            if step == 1 and 0 < at < depth - 1:
                starts.append(("rise", at + 1, 0, 0))
            if step == rounds and at:
                dones.append(("rise", at + 1, 0, 0))
                starts.append(("slab", at - 1))
            stages.append((starts, dones))
    stages += [([("sum",)], [("sum",)])] * (layout.seqs.bit_length() - 1)
    return stages


def body(layout, activations, base_weight, adapter_down, adapter_up, cotangent):
    a, down, up, c = activations[0], adapter_down[0], adapter_up[0], cotangent[0]
    count, depth, width = layout.seqs, layout.depth, activations.shape[2]
    a, c, down, up = (pltpu.with_memory_space_constraint(x, pltpu.HBM) for x in (a, c, down, up))
    scale = adapter_scale / (a.shape[0] * count)

    shifts = [0]
    for step in range(1, depth // 2 + 1):
        shifts += [step] if 2 * step == depth else [step, depth - step]

    here = {("mine", 0, 0): base_weight}
    flying = {}
    state = {}
    flips = [layout.seqs >> step for step in range(1, layout.seqs.bit_length())]
    swapped = set()

    def result_of(name):
        return ("mine", *name[1:3]) if name[0] in ("turn", "rise") else name

    def multiply(at):
        swap_ready(at)
        for name in [name for name in flying if name[0] == "other" and name[1] == at]:
            here[name] = flying.pop(name)
        mine = [here[("mine", at, offset)] for offset in layout.offsets]
        other = [here.pop(("other", at, offset)) for offset in layout.offsets]
        state["acc"], state["grad"] = slab(
            layout, shifts[at], mine, other, a, c, state["low_b"], down, state["low_f"], up,
            state.get("acc"), state.get("grad"), at == 0, at == depth - 1,
        )

    def swap_ready(only=None, most=2):
        names = []
        for side, at, offset in list(here):
            turned = next(o for o in layout.offsets if (o + offset) % count == 0)
            name = ("other", at, turned)
            if side != "mine" or name in swapped or only not in (None, at):
                continue
            if only is None and len(names) == most:
                break
            swapped.add(name)
            flying[name] = layout.swap_cores(here[(side, at, offset)])
            names.append(name)
        return names

    def start(name):
        if name[0] == "local":
            state["low_f"], state["low_b"], state["sum"] = local_terms(a, c, down, up, count)
        elif name[0] == "slab":
            multiply(name[1])
        elif name[0] == "rise":
            _, at, offset, source = name
            shift = (shifts[at] - shifts[source]) % depth
            flying[result_of(name)] = layout.along_depth(here[("mine", source, offset)], shift)
        elif name[0] == "sum":
            flying[name] = layout.across_rank(state["sum"], flips.pop(0))
        else:
            _, at, offset = name
            step = 1 if offset > 0 else -1
            flying[result_of(name)] = layout.along_cycle(here[("mine", at, offset - step)], step)

    def close(names):
        for name in names:
            if name in flying:
                value = flying.pop(name)
                if name[0] == "sum":
                    state["sum"] = state["sum"] + value
                else:
                    here[name] = value
        new_here, new_state = lax.optimization_barrier((dict(here), dict(state)))
        here.update(new_here)
        state.update(new_state)

    for starts, dones in stages_of(layout):
        for name in starts:
            if name[0] not in ("local", "slab"):
                start(name)
        turning = swap_ready()
        for name in starts:
            if name[0] in ("local", "slab"):
                start(name)
        close([result_of(name) for name in dones] + turning)
    multiply(depth - 1)
    sums = state["sum"]
    state["down"], state["up"] = sums[:, :width] * scale, sums[:, width:] * scale
    return tuple(state[name][None] for name in ("acc", "grad", "down", "up"))


def solution(mesh):
    return jax.shard_map(
        functools.partial(body, Layout(mesh)),
        mesh=mesh,
        in_specs=(
            P("blk", "seq", None),
            P("blk", "seq"),
            P("blk", None, None),
            P("blk", None, None),
            P("blk", "seq", None),
        ),
        out_specs=(
            P("blk", "seq", None),
            P("blk", "seq", None),
            P("blk", None, None),
            P("blk", None, None),
        ),
        check_vma=False,
    )
```

```python
import functools

import jax
import jax.numpy as jnp
from jax import lax
from jax.experimental import pallas as pl
from jax.experimental.pallas import tpu as pltpu
from jax.sharding import PartitionSpec as P

adapter_scale = 2.0
axes = ("blk", "seq")
f32 = jnp.float32
bf16 = jnp.bfloat16


def dot(a, b, contract):
    return lax.dot_general(a, b, (contract, ((), ())), preferred_element_type=f32)


class Layout:
    def __init__(self, mesh):
        self.blocks, self.seqs = mesh.shape["blk"], mesh.shape["seq"]
        self.depth = self.blocks // 2
        self.cycle = list(range(0, self.seqs, 2)) + list(range(self.seqs - 1, 0, -2))
        self.place = {seq: at for at, seq in enumerate(self.cycle)}
        self.forward_steps = self.seqs // 2
        self.backward_steps = self.seqs - 1 - self.forward_steps
        self.offsets = [0] + list(range(1, self.forward_steps + 1))
        self.offsets += [-step for step in range(1, self.backward_steps + 1)]

    def permute(self, value, target):
        pairs = []
        for blk in range(self.blocks):
            for seq in range(self.seqs):
                to_blk, to_seq = target(blk // 2, blk % 2, seq)
                pairs.append((blk * self.seqs + seq, to_blk * self.seqs + to_seq))
        return lax.ppermute(value, axes, pairs)

    def along_depth(self, value, shift):
        return self.permute(
            value, lambda z, core, seq: (((z + shift) % self.depth) * 2 + core, seq)
        )

    def along_cycle(self, value, step):
        def target(z, core, seq):
            sign = step if core == 0 else -step
            return z * 2 + core, self.cycle[(self.place[seq] + sign) % self.seqs]

        return self.permute(value, target)

    def swap_cores(self, value):
        return self.permute(value, lambda z, core, seq: (z * 2 + 1 - core, seq))

    def column_of(self, core, seq):
        sign = 1 if core == 0 else -1
        return [
            self.cycle[(self.place[seq] - sign * offset) % self.seqs] for offset in self.offsets
        ]

    def rank(self, core, seq):
        bits = self.seqs.bit_length() - 1
        if core == 1:
            return seq
        return int("".join(reversed(format(seq, f"0{bits}b"))), 2)

    def seq_of_rank(self, core, rank):
        return next(s for s in range(self.seqs) if self.rank(core, s) == rank)

    def across_rank(self, value, flip):
        def target(z, core, seq):
            return z * 2 + core, self.seq_of_rank(core, self.rank(core, seq) ^ flip)

        return self.permute(value, target)


def local_kernel(steps, a_ref, c_ref, down_ref, up_ref, low_f_ref, low_b_ref, grad_ref, acc_ref):
    step = pl.program_id(0)
    width = a_ref.shape[1]

    @pl.when(step == 0)
    def _():
        low_b_ref[...] = dot(c_ref[...], up_ref[...], ((1,), (1,))).astype(bf16)
        acc_ref[...] = jnp.zeros_like(acc_ref)

    block = a_ref[...]
    acc_ref[...] += dot(block, down_ref[...], ((1,), (1,)))
    here = pl.ds(pl.multiple_of(step * width, width), width)
    grad_ref[:, here] = dot(low_b_ref[...], block, ((0,), (0,)))

    @pl.when(step == steps - 1)
    def _():
        low_f = acc_ref[...].astype(bf16)
        low_f_ref[...] = low_f
        grad_ref[:, steps * width :] = dot(low_f, c_ref[...], ((0,), (0,)))


def local_terms(a, c, down, up, steps):
    tokens, width = a.shape
    rank, keys = up.shape
    part = width // steps
    return pl.pallas_call(
        functools.partial(local_kernel, steps),
        grid=(steps,),
        in_specs=[
            pl.BlockSpec((tokens, part), lambda i: (0, i)),
            pl.BlockSpec((tokens, keys), lambda i: (0, 0)),
            pl.BlockSpec((rank, part), lambda i: (0, i)),
            pl.BlockSpec((rank, keys), lambda i: (0, 0)),
        ],
        out_specs=[
            pl.BlockSpec((tokens, rank), lambda i: (0, 0)),
            pl.BlockSpec((tokens, rank), lambda i: (0, 0)),
            pl.BlockSpec((rank, width + keys), lambda i: (0, 0)),
        ],
        out_shape=[
            jax.ShapeDtypeStruct((tokens, rank), bf16),
            jax.ShapeDtypeStruct((tokens, rank), bf16),
            jax.ShapeDtypeStruct((rank, width + keys), f32),
        ],
        scratch_shapes=[pltpu.VMEM((tokens, rank), f32)],
        compiler_params=pltpu.CompilerParams(vmem_limit_bytes=16 << 20),
        cost_estimate=pl.CostEstimate(
            flops=1, bytes_accessed=1, transcendentals=0
        ),
        name="local_terms",
    )(a, c, down, up)


def slab_kernel(layout, shift, first, last, *refs):
    count = layout.seqs
    pieces = [refs[:count], refs[count : 2 * count]]
    a_ref, c_ref, low_b_ref, down_ref, *refs = refs[2 * count :]
    if first:
        low_f_ref, up_ref, *refs = refs
    else:
        acc_in_ref, _, *refs = refs
    keys_ref, grad_ref, panel_ref, rows_a_ref, cot_ref, rows_down_ref, out_ref, *refs = refs
    if last:
        acc_ref, keys_out_ref, keys_sem, *refs = refs
    else:
        acc_ref = keys_ref
    panel_sem, a_sem, cot_sem, down_sem, out_sem = refs
    rows, part = pieces[0][0].shape
    chunks, size = panel_sem.shape[1], out_ref.shape[2]

    blk, seq = lax.axis_index("blk"), lax.axis_index("seq")
    z, core = blk // 2, blk % 2
    source = lax.rem(z + (layout.depth - shift), layout.depth)
    starts = [
        pl.multiple_of((source * 2 + core) * rows, rows),
        pl.multiple_of((source * 2 + 1 - core) * rows, rows),
    ]
    columns = []
    for j in range(count):
        column = jnp.int32(0)
        for k in range(2):
            for s in range(count):
                here = jnp.logical_and(core == k, seq == s)
                column = jnp.where(here, layout.column_of(k, s)[j], column)
        columns.append(pl.ds(pl.multiple_of(column * part, part), part))
    places = [pl.ds(j * part, part) for j in range(count)]

    def cot_copy(j):
        return pltpu.make_async_copy(
            c_ref.at[:, columns[j]], cot_ref.at[:, places[j]], cot_sem.at[j]
        )

    def panel_copy(k, r, j):
        span = pl.ds(r * size, size)
        return pltpu.make_async_copy(
            pieces[k][j].at[span, :], panel_ref.at[k, span, places[j]], panel_sem.at[k, r, j]
        )

    def a_copy(k):
        return pltpu.make_async_copy(
            a_ref.at[:, pl.ds(starts[k], rows)], rows_a_ref.at[k], a_sem.at[k]
        )

    def down_copy(k):
        return pltpu.make_async_copy(
            down_ref.at[:, pl.ds(starts[k], rows)], rows_down_ref.at[k], down_sem.at[k]
        )

    def out_copy(k, r):
        to = pl.ds(pl.multiple_of(starts[k] + r * size, size), size)
        return pltpu.make_async_copy(
            out_ref.at[k * chunks + r], grad_ref.at[:, to], out_sem.at[k, r]
        )

    def keys_copy(j):
        return pltpu.make_async_copy(
            keys_out_ref.at[:, places[j]], keys_ref.at[:, columns[j]], keys_sem.at[j]
        )

    def fetch(k, r):
        for j in range(count):
            panel_copy(k, r, j).start()

    def landed(k, rs=range(chunks)):
        for r in rs:
            for j in range(count):
                panel_copy(k, r, j).wait()

    def frozen_gradient(k, r):
        span = slice(r * size, (r + 1) * size)
        grad = dot(cot_ref[...], panel_ref[k, span, :], ((1,), (1,)))
        grad += dot(low_b, rows_down_ref[k, :, span], ((1,), (0,)))
        out_ref[k * chunks + r] = grad.astype(bf16)
        out_copy(k, r).start()

    def add_keys(k):
        a_copy(k).wait()
        base = acc_ref if first or k else acc_in_ref
        acc_ref[...] = base[...] + dot(rows_a_ref[k], panel_ref[k], ((1,), (0,)))

    for j in range(count):
        cot_copy(j).start()
    for k in range(2):
        down_copy(k).start()
        for r in range(chunks):
            fetch(k, r)
        a_copy(k).start()
    low_b = low_b_ref[...] * jnp.asarray(adapter_scale, bf16)
    if first:
        low_f = low_f_ref[...] * jnp.asarray(adapter_scale, bf16)
        for j in range(count):
            acc_ref[:, places[j]] = dot(low_f, up_ref[:, columns[j]], ((1,), (0,)))
    for j in range(count):
        cot_copy(j).wait()
    for k in range(2):
        down_copy(k).wait()
    for r in range(chunks):
        landed(0, [r])
        frozen_gradient(0, r)
    add_keys(0)
    landed(1)
    if last:
        add_keys(1)
        for j in range(count):
            keys_out_ref[:, places[j]] = acc_ref[:, places[j]].astype(bf16)
            keys_copy(j).start()
    for r in range(chunks):
        frozen_gradient(1, r)
    if last:
        for j in range(count):
            keys_copy(j).wait()
    else:
        add_keys(1)
    for k in range(2):
        for r in range(chunks):
            out_copy(k, r).wait()


def slab(layout, shift, mine, other, a, c, low_b, down, low_f, up, acc, grad, first, last):
    count = len(mine)
    tokens, width = a.shape
    rank, keys = up.shape
    rows = mine[0].shape[0]
    chunks = max(1, rows // 512)
    size = rows // chunks
    whole = pl.BlockSpec(memory_space=pltpu.VMEM)
    remote = pl.BlockSpec(memory_space=pl.ANY)
    in_specs = [remote] * (2 * count + 2) + [whole, remote]
    operands = [*mine, *other, a, c, low_b, down]
    aliases = {}
    if first:
        in_specs += [whole, whole]
        operands += [low_f, up]
    else:
        in_specs += [whole, remote]
        operands += [pltpu.with_memory_space_constraint(acc, pltpu.VMEM), grad]
        aliases = {len(operands) - 1: 1}
        if not last:
            aliases[len(operands) - 2] = 0
    keys_type = jax.ShapeDtypeStruct if last else pltpu.VMEM
    scratch = [
        pltpu.VMEM((2, rows, keys), bf16),
        pltpu.VMEM((2, tokens, rows), bf16),
        pltpu.VMEM((tokens, keys), bf16),
        pltpu.VMEM((2, rank, rows), bf16),
        pltpu.VMEM((2 * chunks, tokens, size), bf16),
    ]
    if last:
        scratch += [
            pltpu.VMEM((tokens, keys), f32),
            pltpu.VMEM((tokens, keys), bf16),
            pltpu.SemaphoreType.DMA((count,)),
        ]
    scratch += [
        pltpu.SemaphoreType.DMA((2, chunks, count)),
        pltpu.SemaphoreType.DMA((2,)),
        pltpu.SemaphoreType.DMA((count,)),
        pltpu.SemaphoreType.DMA((2,)),
        pltpu.SemaphoreType.DMA((2, chunks)),
    ]
    return pl.pallas_call(
        functools.partial(slab_kernel, layout, shift, first, last),
        in_specs=in_specs,
        out_specs=[remote if last else whole, remote],
        scratch_shapes=scratch,
        out_shape=[
            keys_type((tokens, keys), bf16 if last else f32),
            jax.ShapeDtypeStruct((tokens, width), bf16),
        ],
        input_output_aliases=aliases,
        compiler_params=pltpu.CompilerParams(vmem_limit_bytes=24 << 20),
        cost_estimate=pl.CostEstimate(
            flops=1, bytes_accessed=1, transcendentals=0
        ),
        name="slab",
    )(*operands)


def stages_of(layout):
    depth, rounds = layout.depth, layout.forward_steps
    if (depth, layout.seqs) == (4, 4):
        exchanges = [
            ("turn", 0, 1),
            ("turn", 0, -1),
            ("turn", 0, 2),
            ("sum",),
            ("turn", 1, 1),
            ("turn", 1, -1),
            ("turn", 2, 1),
            ("turn", 1, 2),
            ("turn", 2, 2),
            ("turn", 3, 1),
            ("sum",),
            ("turn", 3, 2),
        ]
        besides = {
            0: [("rise", 1, 0, 0), ("local",)],
            2: [("rise", 2, 0, 0)],
            4: [("rise", 3, 0, 1)],
            5: [("slab", 0)],
            6: [("rise", 2, -1, 0)],
            9: [("rise", 3, -1, 1), ("slab", 1)],
            10: [("slab", 2)],
        }
        stages = []
        for at, exchange in enumerate(exchanges):
            starts = exchanges[: 2] if at == 0 else exchanges[at + 1 : at + 2]
            starts = starts + besides.get(at, [])
            dones = [exchange]
            dones += [name for name in besides.get(at - 1, []) if name[0] == "rise"]
            stages.append((starts, dones))
        return stages
    stages = [([("local",), ("rise", 1, 0, 0)], [("rise", 1, 0, 0)])]
    for at in range(depth):
        for step in range(1, rounds + 1):
            starts = [("turn", at, step)]
            if step <= layout.backward_steps:
                starts.append(("turn", at, -step))
            dones = list(starts)
            if step == 1 and 0 < at < depth - 1:
                starts.append(("rise", at + 1, 0, 0))
            if step == rounds and at:
                dones.append(("rise", at + 1, 0, 0))
                starts.append(("slab", at - 1))
            stages.append((starts, dones))
    stages += [([("sum",)], [("sum",)])] * (layout.seqs.bit_length() - 1)
    return stages


def body(layout, activations, base_weight, adapter_down, adapter_up, cotangent):
    a, down, up, c = activations[0], adapter_down[0], adapter_up[0], cotangent[0]
    count, depth, width = layout.seqs, layout.depth, activations.shape[2]
    a, c, down, up = (pltpu.with_memory_space_constraint(x, pltpu.HBM) for x in (a, c, down, up))
    scale = adapter_scale / (a.shape[0] * count)

    shifts = [0]
    for step in range(1, depth // 2 + 1):
        shifts += [step] if 2 * step == depth else [step, depth - step]

    here = {("mine", 0, 0): base_weight}
    flying = {}
    state = {}
    flips = [layout.seqs >> step for step in range(1, layout.seqs.bit_length())]
    swapped = set()

    def result_of(name):
        return ("mine", *name[1:3]) if name[0] in ("turn", "rise") else name

    def multiply(at):
        swap_ready(at)
        for name in [name for name in flying if name[0] == "other" and name[1] == at]:
            here[name] = flying.pop(name)
        mine = [here[("mine", at, offset)] for offset in layout.offsets]
        other = [here.pop(("other", at, offset)) for offset in layout.offsets]
        state["acc"], state["grad"] = slab(
            layout, shifts[at], mine, other, a, c, state["low_b"], down, state["low_f"], up,
            state.get("acc"), state.get("grad"), at == 0, at == depth - 1,
        )

    def swap_ready(only=None, most=2):
        names = []
        for side, at, offset in list(here):
            turned = next(o for o in layout.offsets if (o + offset) % count == 0)
            name = ("other", at, turned)
            if side != "mine" or name in swapped or only not in (None, at):
                continue
            if only is None and len(names) == most:
                break
            swapped.add(name)
            flying[name] = layout.swap_cores(here[(side, at, offset)])
            names.append(name)
        return names

    def start(name):
        if name[0] == "local":
            state["low_f"], state["low_b"], state["sum"] = local_terms(a, c, down, up, count)
        elif name[0] == "slab":
            multiply(name[1])
        elif name[0] == "rise":
            _, at, offset, source = name
            shift = (shifts[at] - shifts[source]) % depth
            flying[result_of(name)] = layout.along_depth(here[("mine", source, offset)], shift)
        elif name[0] == "sum":
            flying[name] = layout.across_rank(state["sum"], flips.pop(0))
        else:
            _, at, offset = name
            step = 1 if offset > 0 else -1
            flying[result_of(name)] = layout.along_cycle(here[("mine", at, offset - step)], step)

    def close(names):
        for name in names:
            if name in flying:
                value = flying.pop(name)
                if name[0] == "sum":
                    state["sum"] = state["sum"] + value
                else:
                    here[name] = value
        new_here, new_state = lax.optimization_barrier((dict(here), dict(state)))
        here.update(new_here)
        state.update(new_state)

    for starts, dones in stages_of(layout):
        for name in starts:
            if name[0] not in ("local", "slab"):
                start(name)
        turning = swap_ready()
        for name in starts:
            if name[0] in ("local", "slab"):
                start(name)
        close([result_of(name) for name in dones] + turning)
    multiply(depth - 1)
    sums = state["sum"]
    state["down"], state["up"] = sums[:, :width] * scale, sums[:, width:] * scale
    return tuple(state[name][None] for name in ("acc", "grad", "down", "up"))


def solution(mesh):
    return jax.shard_map(
        functools.partial(body, Layout(mesh)),
        mesh=mesh,
        in_specs=(
            P("blk", "seq", None),
            P("blk", "seq"),
            P("blk", None, None),
            P("blk", None, None),
            P("blk", "seq", None),
        ),
        out_specs=(
            P("blk", "seq", None),
            P("blk", "seq", None),
            P("blk", None, None),
            P("blk", None, None),
        ),
        check_vma=False,
    )
```

```python
import functools

import jax
import jax.numpy as jnp
from jax import lax
from jax.experimental import pallas as pl
from jax.experimental.pallas import tpu as pltpu
from jax.sharding import PartitionSpec as P

adapter_scale = 2.0
axes = ("blk", "seq")
f32 = jnp.float32
bf16 = jnp.bfloat16


def dot(a, b, contract):
    return lax.dot_general(a, b, (contract, ((), ())), preferred_element_type=f32)


class Layout:
    def __init__(self, mesh):
        self.blocks, self.seqs = mesh.shape["blk"], mesh.shape["seq"]
        self.depth = self.blocks // 2
        self.cycle = list(range(0, self.seqs, 2)) + list(range(self.seqs - 1, 0, -2))
        self.place = {seq: at for at, seq in enumerate(self.cycle)}
        self.forward_steps = self.seqs // 2
        self.backward_steps = self.seqs - 1 - self.forward_steps
        self.offsets = [0] + list(range(1, self.forward_steps + 1))
        self.offsets += [-step for step in range(1, self.backward_steps + 1)]

    def permute(self, value, target):
        pairs = []
        for blk in range(self.blocks):
            for seq in range(self.seqs):
                to_blk, to_seq = target(blk // 2, blk % 2, seq)
                pairs.append((blk * self.seqs + seq, to_blk * self.seqs + to_seq))
        return lax.ppermute(value, axes, pairs)

    def along_depth(self, value, shift):
        return self.permute(
            value, lambda z, core, seq: (((z + shift) % self.depth) * 2 + core, seq)
        )

    def along_cycle(self, value, step):
        def target(z, core, seq):
            sign = step if core == 0 else -step
            return z * 2 + core, self.cycle[(self.place[seq] + sign) % self.seqs]

        return self.permute(value, target)

    def swap_cores(self, value):
        return self.permute(value, lambda z, core, seq: (z * 2 + 1 - core, seq))

    def column_of(self, core, seq):
        sign = 1 if core == 0 else -1
        return [
            self.cycle[(self.place[seq] - sign * offset) % self.seqs] for offset in self.offsets
        ]

    def rank(self, core, seq):
        bits = self.seqs.bit_length() - 1
        if core == 1:
            return seq
        return int("".join(reversed(format(seq, f"0{bits}b"))), 2)

    def seq_of_rank(self, core, rank):
        return next(s for s in range(self.seqs) if self.rank(core, s) == rank)

    def across_rank(self, value, flip):
        def target(z, core, seq):
            return z * 2 + core, self.seq_of_rank(core, self.rank(core, seq) ^ flip)

        return self.permute(value, target)


def local_kernel(steps, a_ref, c_ref, down_ref, up_ref, low_f_ref, low_b_ref, grad_ref, acc_ref):
    step = pl.program_id(0)
    width = a_ref.shape[1]

    @pl.when(step == 0)
    def _():
        low_b_ref[...] = dot(c_ref[...], up_ref[...], ((1,), (1,))).astype(bf16)
        acc_ref[...] = jnp.zeros_like(acc_ref)

    block = a_ref[...]
    acc_ref[...] += dot(block, down_ref[...], ((1,), (1,)))
    here = pl.ds(pl.multiple_of(step * width, width), width)
    grad_ref[:, here] = dot(low_b_ref[...], block, ((0,), (0,)))

    @pl.when(step == steps - 1)
    def _():
        low_f = acc_ref[...].astype(bf16)
        low_f_ref[...] = low_f
        grad_ref[:, steps * width :] = dot(low_f, c_ref[...], ((0,), (0,)))


def local_terms(a, c, down, up, steps):
    tokens, width = a.shape
    rank, keys = up.shape
    part = width // steps
    return pl.pallas_call(
        functools.partial(local_kernel, steps),
        grid=(steps,),
        in_specs=[
            pl.BlockSpec((tokens, part), lambda i: (0, i)),
            pl.BlockSpec((tokens, keys), lambda i: (0, 0)),
            pl.BlockSpec((rank, part), lambda i: (0, i)),
            pl.BlockSpec((rank, keys), lambda i: (0, 0)),
        ],
        out_specs=[
            pl.BlockSpec((tokens, rank), lambda i: (0, 0)),
            pl.BlockSpec((tokens, rank), lambda i: (0, 0)),
            pl.BlockSpec((rank, width + keys), lambda i: (0, 0)),
        ],
        out_shape=[
            jax.ShapeDtypeStruct((tokens, rank), bf16),
            jax.ShapeDtypeStruct((tokens, rank), bf16),
            jax.ShapeDtypeStruct((rank, width + keys), f32),
        ],
        scratch_shapes=[pltpu.VMEM((tokens, rank), f32)],
        compiler_params=pltpu.CompilerParams(vmem_limit_bytes=16 << 20),
        cost_estimate=pl.CostEstimate(
            flops=1, bytes_accessed=1, transcendentals=0
        ),
        name="local_terms",
    )(a, c, down, up)


def slab_kernel(layout, shift, first, last, *refs):
    count = layout.seqs
    pieces = [refs[:count], refs[count : 2 * count]]
    a_ref, c_ref, low_b_ref, down_ref, *refs = refs[2 * count :]
    if first:
        low_f_ref, up_ref, *refs = refs
    else:
        acc_in_ref, _, *refs = refs
    keys_ref, grad_ref, panel_ref, rows_a_ref, cot_ref, rows_down_ref, out_ref, *refs = refs
    if last:
        acc_ref, keys_out_ref, keys_sem, *refs = refs
    else:
        acc_ref = keys_ref
    panel_sem, a_sem, cot_sem, down_sem, out_sem = refs
    rows, part = pieces[0][0].shape
    chunks, size = panel_sem.shape[1], out_ref.shape[2]

    blk, seq = lax.axis_index("blk"), lax.axis_index("seq")
    z, core = blk // 2, blk % 2
    source = lax.rem(z + (layout.depth - shift), layout.depth)
    starts = [
        pl.multiple_of((source * 2 + core) * rows, rows),
        pl.multiple_of((source * 2 + 1 - core) * rows, rows),
    ]
    columns = []
    for j in range(count):
        column = jnp.int32(0)
        for k in range(2):
            for s in range(count):
                here = jnp.logical_and(core == k, seq == s)
                column = jnp.where(here, layout.column_of(k, s)[j], column)
        columns.append(pl.ds(pl.multiple_of(column * part, part), part))
    places = [pl.ds(j * part, part) for j in range(count)]

    def cot_copy(j):
        return pltpu.make_async_copy(
            c_ref.at[:, columns[j]], cot_ref.at[:, places[j]], cot_sem.at[j]
        )

    def panel_copy(k, r, j):
        span = pl.ds(r * size, size)
        return pltpu.make_async_copy(
            pieces[k][j].at[span, :], panel_ref.at[k, span, places[j]], panel_sem.at[k, r, j]
        )

    def a_copy(k):
        return pltpu.make_async_copy(
            a_ref.at[:, pl.ds(starts[k], rows)], rows_a_ref.at[k], a_sem.at[k]
        )

    def down_copy(k):
        return pltpu.make_async_copy(
            down_ref.at[:, pl.ds(starts[k], rows)], rows_down_ref.at[k], down_sem.at[k]
        )

    def out_copy(k, r):
        to = pl.ds(pl.multiple_of(starts[k] + r * size, size), size)
        return pltpu.make_async_copy(
            out_ref.at[k * chunks + r], grad_ref.at[:, to], out_sem.at[k, r]
        )

    def keys_copy(j):
        return pltpu.make_async_copy(
            keys_out_ref.at[:, places[j]], keys_ref.at[:, columns[j]], keys_sem.at[j]
        )

    def fetch(k, r):
        for j in range(count):
            panel_copy(k, r, j).start()

    def landed(k, rs=range(chunks)):
        for r in rs:
            for j in range(count):
                panel_copy(k, r, j).wait()

    def frozen_gradient(k, r):
        span = slice(r * size, (r + 1) * size)
        grad = dot(cot_ref[...], panel_ref[k, span, :], ((1,), (1,)))
        grad += dot(low_b, rows_down_ref[k, :, span], ((1,), (0,)))
        out_ref[k * chunks + r] = grad.astype(bf16)
        out_copy(k, r).start()

    def add_keys(k):
        a_copy(k).wait()
        base = acc_ref if first or k else acc_in_ref
        acc_ref[...] = base[...] + dot(rows_a_ref[k], panel_ref[k], ((1,), (0,)))

    for j in range(count):
        cot_copy(j).start()
    for k in range(2):
        down_copy(k).start()
        for r in range(chunks):
            fetch(k, r)
        a_copy(k).start()
    low_b = low_b_ref[...] * jnp.asarray(adapter_scale, bf16)
    if first:
        low_f = low_f_ref[...] * jnp.asarray(adapter_scale, bf16)
        for j in range(count):
            acc_ref[:, places[j]] = dot(low_f, up_ref[:, columns[j]], ((1,), (0,)))
    for j in range(count):
        cot_copy(j).wait()
    for k in range(2):
        down_copy(k).wait()
    for r in range(chunks):
        landed(0, [r])
        frozen_gradient(0, r)
    add_keys(0)
    landed(1)
    if last:
        add_keys(1)
        for j in range(count):
            keys_out_ref[:, places[j]] = acc_ref[:, places[j]].astype(bf16)
            keys_copy(j).start()
    for r in range(chunks):
        frozen_gradient(1, r)
    if last:
        for j in range(count):
            keys_copy(j).wait()
    else:
        add_keys(1)
    for k in range(2):
        for r in range(chunks):
            out_copy(k, r).wait()


def slab(layout, shift, mine, other, a, c, low_b, down, low_f, up, acc, grad, first, last):
    count = len(mine)
    tokens, width = a.shape
    rank, keys = up.shape
    rows = mine[0].shape[0]
    chunks = max(1, rows // 512)
    size = rows // chunks
    whole = pl.BlockSpec(memory_space=pltpu.VMEM)
    remote = pl.BlockSpec(memory_space=pl.ANY)
    in_specs = [remote] * (2 * count + 2) + [whole, remote]
    operands = [*mine, *other, a, c, low_b, down]
    aliases = {}
    if first:
        in_specs += [whole, whole]
        operands += [low_f, up]
    else:
        in_specs += [whole, remote]
        operands += [pltpu.with_memory_space_constraint(acc, pltpu.VMEM), grad]
        aliases = {len(operands) - 1: 1}
        if not last:
            aliases[len(operands) - 2] = 0
    keys_type = jax.ShapeDtypeStruct if last else pltpu.VMEM
    scratch = [
        pltpu.VMEM((2, rows, keys), bf16),
        pltpu.VMEM((2, tokens, rows), bf16),
        pltpu.VMEM((tokens, keys), bf16),
        pltpu.VMEM((2, rank, rows), bf16),
        pltpu.VMEM((2 * chunks, tokens, size), bf16),
    ]
    if last:
        scratch += [
            pltpu.VMEM((tokens, keys), f32),
            pltpu.VMEM((tokens, keys), bf16),
            pltpu.SemaphoreType.DMA((count,)),
        ]
    scratch += [
        pltpu.SemaphoreType.DMA((2, chunks, count)),
        pltpu.SemaphoreType.DMA((2,)),
        pltpu.SemaphoreType.DMA((count,)),
        pltpu.SemaphoreType.DMA((2,)),
        pltpu.SemaphoreType.DMA((2, chunks)),
    ]
    return pl.pallas_call(
        functools.partial(slab_kernel, layout, shift, first, last),
        in_specs=in_specs,
        out_specs=[remote if last else whole, remote],
        scratch_shapes=scratch,
        out_shape=[
            keys_type((tokens, keys), bf16 if last else f32),
            jax.ShapeDtypeStruct((tokens, width), bf16),
        ],
        input_output_aliases=aliases,
        compiler_params=pltpu.CompilerParams(vmem_limit_bytes=24 << 20),
        cost_estimate=pl.CostEstimate(
            flops=1, bytes_accessed=1, transcendentals=0
        ),
        name="slab",
    )(*operands)


def stages_of(layout):
    depth, rounds = layout.depth, layout.forward_steps
    if (depth, layout.seqs) == (4, 4):
        exchanges = [
            ("turn", 0, 1),
            ("turn", 0, -1),
            ("turn", 0, 2),
            ("sum",),
            ("turn", 1, 1),
            ("turn", 1, -1),
            ("turn", 2, 1),
            ("turn", 1, 2),
            ("turn", 2, 2),
            ("turn", 3, 1),
            ("sum",),
            ("turn", 3, 2),
        ]
        besides = {
            0: [("rise", 1, 0, 0), ("local",)],
            2: [("rise", 2, 0, 0)],
            4: [("rise", 3, 0, 1)],
            5: [("slab", 0)],
            7: [("rise", 2, -1, 0)],
            9: [("rise", 3, -1, 1), ("slab", 1)],
            10: [("slab", 2)],
        }
        stages = []
        for at, exchange in enumerate(exchanges):
            starts = exchanges[: 2] if at == 0 else exchanges[at + 1 : at + 2]
            starts = starts + besides.get(at, [])
            dones = [exchange]
            dones += [name for name in besides.get(at - 1, []) if name[0] == "rise"]
            stages.append((starts, dones))
        return stages
    stages = [([("local",), ("rise", 1, 0, 0)], [("rise", 1, 0, 0)])]
    for at in range(depth):
        for step in range(1, rounds + 1):
            starts = [("turn", at, step)]
            if step <= layout.backward_steps:
                starts.append(("turn", at, -step))
            dones = list(starts)
            if step == 1 and 0 < at < depth - 1:
                starts.append(("rise", at + 1, 0, 0))
            if step == rounds and at:
                dones.append(("rise", at + 1, 0, 0))
                starts.append(("slab", at - 1))
            stages.append((starts, dones))
    stages += [([("sum",)], [("sum",)])] * (layout.seqs.bit_length() - 1)
    return stages


def body(layout, activations, base_weight, adapter_down, adapter_up, cotangent):
    a, down, up, c = activations[0], adapter_down[0], adapter_up[0], cotangent[0]
    count, depth, width = layout.seqs, layout.depth, activations.shape[2]
    a, c, down, up = (pltpu.with_memory_space_constraint(x, pltpu.HBM) for x in (a, c, down, up))
    scale = adapter_scale / (a.shape[0] * count)

    shifts = [0]
    for step in range(1, depth // 2 + 1):
        shifts += [step] if 2 * step == depth else [step, depth - step]

    here = {("mine", 0, 0): base_weight}
    flying = {}
    state = {}
    flips = [layout.seqs >> step for step in range(1, layout.seqs.bit_length())]
    swapped = set()

    def result_of(name):
        return ("mine", *name[1:3]) if name[0] in ("turn", "rise") else name

    def multiply(at):
        swap_ready(at)
        for name in [name for name in flying if name[0] == "other" and name[1] == at]:
            here[name] = flying.pop(name)
        mine = [here[("mine", at, offset)] for offset in layout.offsets]
        other = [here.pop(("other", at, offset)) for offset in layout.offsets]
        state["acc"], state["grad"] = slab(
            layout, shifts[at], mine, other, a, c, state["low_b"], down, state["low_f"], up,
            state.get("acc"), state.get("grad"), at == 0, at == depth - 1,
        )

    def swap_ready(only=None, most=2):
        names = []
        for side, at, offset in list(here):
            turned = next(o for o in layout.offsets if (o + offset) % count == 0)
            name = ("other", at, turned)
            if side != "mine" or name in swapped or only not in (None, at):
                continue
            if only is None and len(names) == most:
                break
            swapped.add(name)
            flying[name] = layout.swap_cores(here[(side, at, offset)])
            names.append(name)
        return names

    def start(name):
        if name[0] == "local":
            state["low_f"], state["low_b"], state["sum"] = local_terms(a, c, down, up, count)
        elif name[0] == "slab":
            multiply(name[1])
        elif name[0] == "rise":
            _, at, offset, source = name
            shift = (shifts[at] - shifts[source]) % depth
            flying[result_of(name)] = layout.along_depth(here[("mine", source, offset)], shift)
        elif name[0] == "sum":
            flying[name] = layout.across_rank(state["sum"], flips.pop(0))
        else:
            _, at, offset = name
            step = 1 if offset > 0 else -1
            flying[result_of(name)] = layout.along_cycle(here[("mine", at, offset - step)], step)

    def close(names):
        for name in names:
            if name in flying:
                value = flying.pop(name)
                if name[0] == "sum":
                    state["sum"] = state["sum"] + value
                else:
                    here[name] = value
        new_here, new_state = lax.optimization_barrier((dict(here), dict(state)))
        here.update(new_here)
        state.update(new_state)

    for starts, dones in stages_of(layout):
        for name in starts:
            if name[0] not in ("local", "slab"):
                start(name)
        turning = swap_ready()
        for name in starts:
            if name[0] in ("local", "slab"):
                start(name)
        close([result_of(name) for name in dones] + turning)
    multiply(depth - 1)
    sums = state["sum"]
    state["down"], state["up"] = sums[:, :width] * scale, sums[:, width:] * scale
    return tuple(state[name][None] for name in ("acc", "grad", "down", "up"))


def solution(mesh):
    return jax.shard_map(
        functools.partial(body, Layout(mesh)),
        mesh=mesh,
        in_specs=(
            P("blk", "seq", None),
            P("blk", "seq"),
            P("blk", None, None),
            P("blk", None, None),
            P("blk", "seq", None),
        ),
        out_specs=(
            P("blk", "seq", None),
            P("blk", "seq", None),
            P("blk", None, None),
            P("blk", None, None),
        ),
        check_vma=False,
    )
```
